128 devices in a mesh: gx: 16 (over y, z), gy: 8 (over x, core).
Axes of the slice: x: 4, y: 4, z: 4, core: 2. Of those that a mesh axis runs over, the one named last changes fastest.
Arguments:
- destination: int32 [32768, 1], P(('gx', 'gy')), may hold values from 0 to 127; in each aligned block of 256 rows (0 to 255, 256 to 511, ...) at most 3 rows name the same one
- row_count: int32 [32768], P(('gx', 'gy')), may hold values from 1 to 128
- old_cell: int32 [32768, 128], P(('gx', 'gy')), may hold values from 0 to 4095
- new_cell: int32 [32768, 128], P(('gx', 'gy')), may hold values from 0 to 4095
- point_mass: float32 [32768, 128], P(('gx', 'gy')), may hold values from 0.5 to 2
- point_vel: float32 [32768, 3, 128], P(('gx', 'gy')), may hold values from -6 to 6
- grid_delta: float32 [3, 128, 4, 1024], P(None, 'gx', None, 'gy'), may hold values from -6 to 6
- fluid_mass: float32 [128, 4, 1024], P('gx', None, 'gy'), may hold values from 0.5 to 2
- fluid_momentum: float32 [3, 128, 4, 1024], P(None, 'gx', None, 'gy'), may hold values from -6 to 6
Outputs:
- coupled_cell_velocity: float32 [3, 128, 4, 1024], P(None, 'gx', None, 'gy')
- pressure: float32 [128, 4, 1024], P('gx', None, 'gy')
The draws below stay inside these ranges and needn't reach their ends.
Inputs may be any that keep to these rules, and one draw needn't show every extreme that they name: destination numbers owners gx * 8 + gy; the rows of one device send at most 3 rows to one owner. `row_count`: lanes at or above a row's count are padding.
All inputs are finite; a program needn't handle non-finite values.
Results may differ from the reference program's by a relative error of at most 0.00014.
Values sent between devices are 32-bit elements; how exact they have to be, the bound alone decides.
No kernel may reach another device: no remote copies, remote signals or barrier semaphores. Data moves between devices by JAX's collectives and lax.ppermute only.
A program may use at most 64 MiB of HBM per device.

```python
import math
import jax
import jax.numpy as jnp
import numpy as np
from jax import lax

PR = 128
ROWS_DEV = 256
CX = 8
CY = 128
CZ = 4
SWEEPS = 4
OWNERS = 128
CAP = 3
ROW_TOTAL = 32768
CELLS_DEV = 4096
NX = 128
NY = 1024
N_GY = 8


def with_ends(entries, stream_key, low, top_value):
    longest = entries.shape.index(max(entries.shape))
    spots = []
    for shift in (0, 1):
        where = [jax.random.randint(jax.random.fold_in(stream_key, axis), (), 0, length) for axis, length in enumerate(entries.shape)]
        where[longest] = (where[longest] + shift) % entries.shape[longest]
        spots.append(tuple(where))
    return entries.at[spots[0]].set(low).at[spots[1]].set(top_value)


def block_levels(rng, extent, shards, least, largest):
    level = 1.0
    for position, blocks in shards:
        draws = jax.random.uniform(jax.random.fold_in(jax.random.fold_in(rng, 6), position), (blocks,), jnp.float32, least / len(shards), largest / len(shards))
        level = level * jnp.repeat(jnp.exp(draws), extent[position] // blocks).reshape((-1,) + (1,) * (len(extent) - 1 - position))
    return level


def shared_out(stream_key, own, number, rows, number_of, top, bound, lean):
    sequence = jax.random.permutation(stream_key, number_of)
    heavy_load, usual = shares(number_of, rows * top, bound, lean, True), shares(number_of, rows * top, bound, lean, False)
    places = jnp.arange(number_of)

    def named(tallies, turn):
        used = int((tallies > 0).sum())
        fixed = max(1, used // 4)
        moved = fixed + (places - fixed + turn * (used - fixed)) % max(1, number_of - fixed)
        return jnp.zeros((number_of,), jnp.int32).at[sequence[jnp.where(places < fixed, places, moved)]].set(jnp.asarray(tallies, jnp.int32))

    tallies = jnp.where(number % 4 == 0, named(heavy_load, number // 4), named(usual, number - number // 4 - 1))
    mixed = jax.random.permutation(jax.random.fold_in(own, 3), number_of)
    donor, receiver = mixed[0:number_of // 2 * 2:2], mixed[1:number_of // 2 * 2:2]
    slack = jnp.minimum(tallies[donor] - 1, bound - tallies[receiver]) // 2
    slack = jnp.where((donor == sequence[0]) | (receiver == sequence[0]) | (tallies[receiver] == 0), 0, jnp.maximum(slack, 0))
    moved = jax.random.randint(jax.random.fold_in(own, 4), (number_of // 2,), 0, 1 << 20) % (slack + 1)
    tallies = tallies.at[donor].add(-moved).at[receiver].add(moved)
    labels = jnp.searchsorted(jnp.cumsum(tallies), jnp.arange(rows * top), side="right").astype(jnp.int32)
    grid = labels.reshape(top, rows).T
    grid = grid[jax.random.permutation(jax.random.fold_in(own, 1), rows)]
    turn = jax.random.randint(jax.random.fold_in(own, 2), (rows, 1), 0, top)
    return jnp.take_along_axis(grid, (jnp.arange(top)[None, :] + turn) % top, axis=1)


def shares(count, total, bound, lean, full):
    weights = [(1 << 20) // math.isqrt(grade ** lean) + 1 for grade in range(1, count + 1)]
    largest = bound if full else min(bound, max(-(-total // count), total * weights[0] // sum(weights)))
    least = 1 if total - largest >= count - 1 else 0
    counts, surplus = [largest] + [least] * (count - 1), total - largest - least * (count - 1)
    while surplus > 0:
        candidates = [i for i in range(1, count) if counts[i] < largest] or [i for i in range(1, count) if counts[i] < bound]
        whole, left = sum([weights[i] for i in candidates]), surplus
        for i in candidates:
            extra = min(bound - counts[i], max(1, left * weights[i] // whole), surplus)
            counts[i] = counts[i] + extra
            surplus = surplus - extra
    return np.array(counts)


def noise(rng, shape, deviation, limit, pieces=(), dtype=jnp.bfloat16):
    result = jax.random.normal(rng, shape, jnp.float32) * deviation
    if len(pieces) > 0:
        result = block_levels(rng, shape, pieces, -0.22, 0.18) * result
    return jnp.clip(result, min=-limit, max=limit).astype(dtype)


def setup_inputs(seed: int = 0) -> dict:
    key_of = jax.random.split(jax.random.key(seed), 10)
    destination_keys = jax.random.split(jax.random.fold_in(key_of[0], 1), ROW_TOTAL // ROWS_DEV)
    destination_turns = jax.random.permutation(jax.random.fold_in(key_of[0], 3), ROW_TOTAL // ROWS_DEV)
    destination = jax.vmap(lambda own, number: shared_out(jax.random.fold_in(key_of[0], 2), own, number, ROWS_DEV, OWNERS, 1, CAP, 2))(destination_keys, destination_turns).reshape((ROW_TOTAL, 1))
    row_count = with_ends(jax.random.randint(key_of[1], (ROW_TOTAL,), 1, PR + 1), jax.random.fold_in(key_of[1], 1), 1, PR).astype(jnp.int32)
    old_cell = with_ends(jax.random.randint(key_of[2], (ROW_TOTAL, PR), 0, CELLS_DEV), jax.random.fold_in(key_of[2], 1), 0, CELLS_DEV - 1).astype(jnp.int32)
    new_cell = with_ends(jax.random.randint(key_of[3], (ROW_TOTAL, PR), 0, CELLS_DEV), jax.random.fold_in(key_of[3], 1), 0, CELLS_DEV - 1).astype(jnp.int32)
    point_mass = jnp.clip(jnp.exp(math.log(2.0) - 1.3862944 * jax.random.uniform(key_of[4], (ROW_TOTAL, PR), jnp.float32) ** block_levels(key_of[4], (ROW_TOTAL, PR), ((0, 128),), -0.2, 0.2)), 0.5, 2.0)
    point_vel = noise(key_of[5], (ROW_TOTAL, 3, PR), 1.0, 6.0, ((0, 128),), jnp.float32)
    grid_delta = noise(key_of[6], (3, NX, CZ, NY), 1.0, 6.0, ((1, 16), (3, 8)), jnp.float32)
    fluid_mass = jnp.clip(jnp.exp(math.log(2.0) - 1.3862944 * jax.random.uniform(key_of[7], (NX, CZ, NY), jnp.float32) ** block_levels(key_of[7], (NX, CZ, NY), ((0, 16), (2, 8)), -0.2, 0.2)), 0.5, 2.0)
    fluid_momentum = noise(key_of[8], (3, NX, CZ, NY), 1.0, 6.0, ((1, 16), (3, 8)), jnp.float32)
    return {"destination": destination, "row_count": row_count, "old_cell": old_cell, "new_cell": new_cell, "point_mass": point_mass, "point_vel": point_vel, "grid_delta": grid_delta, "fluid_mass": fluid_mass, "fluid_momentum": fluid_momentum}


eigen_low = 0.5
eigen_high = 14.5


def neighbour_sum(field):
    padded = jnp.pad(field, 1)
    return (padded[2:, 1:-1, 1:-1] + padded[:-2, 1:-1, 1:-1] + padded[1:-1, 2:, 1:-1]
            + padded[1:-1, :-2, 1:-1] + padded[1:-1, 1:-1, 2:] + padded[1:-1, 1:-1, :-2])


def global_index(owner, cell):
    owner_x = owner // N_GY
    owner_y = owner % N_GY
    across = cell // (CZ * CY)
    depth = (cell // CY) % CZ
    along = cell % CY
    return ((owner_x * CX + across) * CZ + depth) * NY + owner_y * CY + along


def reference(destination, row_count, old_cell, new_cell, point_mass, point_vel, grid_delta, fluid_mass, fluid_momentum):
    row_total = destination.shape[0]
    anchor = lax.broadcasted_iota(jnp.int32, (row_total, 1), 0) // ROWS_DEV
    lane_index = lax.broadcasted_iota(jnp.int32, (row_total, PR), 1)
    live = lane_index < row_count[:, None]
    mass = jnp.where(live, point_mass, jnp.float32(0.0))
    old_index = global_index(anchor, old_cell).reshape(-1)
    new_index = global_index(destination, new_cell).reshape(-1)
    cell_total = NX * CZ * NY
    delta_flat = grid_delta.reshape(3, cell_total)
    mass_sum = jax.ops.segment_sum(mass.reshape(-1), new_index, cell_total).reshape(NX, CZ, NY)
    sums = []
    for component in range(3):
        velocity_new = point_vel[:, component, :] + delta_flat[component][old_index].reshape(row_total, PR)
        sums.append(jax.ops.segment_sum((mass * velocity_new).reshape(-1), new_index, cell_total))
    momentum_sum = jnp.stack(sums, 0).reshape(3, NX, CZ, NY)
    total_mass = fluid_mass + mass_sum
    coupled_cell_velocity = (fluid_momentum + momentum_sum) / total_mass
    stiffness = 0.5 + 1.0 / total_mass
    padded_x_velocity = jnp.pad(coupled_cell_velocity[0], ((1, 1), (0, 0), (0, 0)))
    padded_y_velocity = jnp.pad(coupled_cell_velocity[1], ((0, 0), (0, 0), (1, 1)))
    padded_z_velocity = jnp.pad(coupled_cell_velocity[2], ((0, 0), (1, 1), (0, 0)))
    sending_rank = -0.5 * ((padded_x_velocity[2:] - padded_x_velocity[:-2]) + (padded_y_velocity[:, :, 2:] - padded_y_velocity[:, :, :-2]) + (padded_z_velocity[:, 2:] - padded_z_velocity[:, :-2]))
    theta = (eigen_high + eigen_low) / 2.0
    delta = (eigen_high - eigen_low) / 2.0
    sigma = theta / delta
    rho = 1.0 / sigma
    pressure = jnp.zeros_like(sending_rank)
    residual = sending_rank
    search = sending_rank / theta
    for sweep in range(SWEEPS):
        pressure = pressure + search
        if sweep + 1 < SWEEPS:
            residual = residual - ((6.0 + stiffness) * search - neighbour_sum(search))
            rho_new = 1.0 / (2.0 * sigma - rho)
            search = rho_new * rho * search + (2.0 * rho_new / delta) * residual
            rho = rho_new
    return coupled_cell_velocity, pressure
```

```python
import jax
import jax.numpy as jnp
from jax import lax
from jax.experimental import pallas as pl
from jax.experimental.pallas import tpu as pltpu
from jax.sharding import PartitionSpec as P

CAP = 3
FIELDS = 5
SWEEPS = 4
WIDTH = 4

eigen_low = 0.5
eigen_high = 14.5


def pieces(value):
    top = value.astype(jnp.bfloat16)
    rest = value - top.astype(jnp.float32)
    middle = rest.astype(jnp.bfloat16)
    bottom = (rest - middle.astype(jnp.float32)).astype(jnp.bfloat16)
    return top, middle, bottom


def pack_kernel(target_ref, count_ref, old_ref, new_ref, mass_ref, vel_ref, delta_ref, out_ref, live_ref, pay_ref):
    rows, lanes = mass_ref.shape
    owners = out_ref.shape[0] // (CAP * FIELDS)
    levels = delta_ref.shape[0] // 3
    lane_index = lax.broadcasted_iota(jnp.int32, (lanes, lanes), 1)
    for part in range(rows // lanes):
        band = slice(part * lanes, (part + 1) * lanes)
        counts = jnp.broadcast_to(count_ref[:, band].astype(jnp.float32), (lanes, lanes)).T
        live_ref[band, :] = jnp.where(lane_index.astype(jnp.float32) < counts, mass_ref[band, :], 0.0)

    step = 16

    def gather(index, carry):
        band = pl.ds(pl.multiple_of(index * step, step), step)
        cell = old_ref[band, :]
        along = cell & (lanes - 1)
        level = cell >> 7
        found = [jnp.zeros((step, lanes), jnp.float32)] * 3
        for h in range(levels):
            mask = level == h
            for c in range(3):
                table = jnp.broadcast_to(delta_ref[c * levels + h : c * levels + h + 1, :], (step, lanes))
                picked = jnp.take_along_axis(table, along, axis=1)
                found[c] = jnp.where(mask, picked, found[c])
        mass = live_ref[band, :]
        parts = [mass] + [mass * (vel_ref[c, band, :] + found[c]) for c in range(3)]
        parts.append(new_ref[band, :].astype(jnp.float32))
        for f, part in enumerate(parts):
            for k, piece in enumerate(pieces(part)):
                pay_ref[pl.ds(pl.multiple_of(k * rows + index * step, step), step), f * lanes : (f + 1) * lanes] = piece
        return carry

    lax.fori_loop(0, rows // step, gather, 0)

    target = jnp.broadcast_to(target_ref[...], (owners, rows))
    marks = target == lax.broadcasted_iota(jnp.int32, (owners, rows), 0)
    before = lax.broadcasted_iota(jnp.int32, (rows, rows), 0) < lax.broadcasted_iota(jnp.int32, (rows, rows), 1)
    ones = jnp.where(marks, 1.0, 0.0)
    earlier = jnp.dot(ones.astype(jnp.bfloat16), jnp.where(before, 1.0, 0.0).astype(jnp.bfloat16), preferred_element_type=jnp.float32)
    for s in range(CAP):
        chosen = jnp.where(earlier == float(s), ones, 0.0).astype(jnp.bfloat16)
        picked = jnp.dot(jnp.concatenate([chosen] * 3, axis=1), pay_ref[...], preferred_element_type=jnp.float32)
        for f in range(FIELDS):
            out_ref[pl.ds(f * CAP + s, owners, stride=CAP * FIELDS), :] = picked[:, f * lanes : (f + 1) * lanes]


def pack(target, count, old_cell, new_cell, point_mass, point_vel, delta):
    rows, lanes = point_mass.shape
    owners = lax.axis_size("gx") * lax.axis_size("gy")
    return pl.pallas_call(
        pack_kernel,
        out_shape=jax.ShapeDtypeStruct((owners * CAP * FIELDS, lanes), jnp.float32),
        scratch_shapes=[
            pltpu.VMEM((rows, lanes), jnp.float32),
            pltpu.VMEM((3 * rows, FIELDS * lanes), jnp.bfloat16),
        ],
        name="pack",
    )(target, count, old_cell, new_cell, point_mass, point_vel, delta)


def deposit_kernel(in_ref, mass_ref, momentum_ref, vel_ref, field_ref, strip_ref, acc_ref):
    lanes = in_ref.shape[1]
    levels = mass_ref.shape[0]
    sources = in_ref.shape[0] // (CAP * FIELDS)
    group = 2
    acc_ref[...] = jnp.zeros_like(acc_ref)
    along_index = lax.broadcasted_iota(jnp.int32, (lanes, lanes), 0)
    level_index = lax.broadcasted_iota(jnp.int32, (levels, lanes), 0)

    def add(index, carry):
        lefts, rights = [], []
        for g in range(group):
            base = (index * group + g) * (CAP * FIELDS)
            for s in range(CAP):
                row = lambda f: in_ref[pl.ds(base + f * CAP + s, 1), :]
                cell = row(4).astype(jnp.int32)
                along = jnp.broadcast_to(cell & (lanes - 1), (lanes, lanes))
                level = jnp.broadcast_to(cell >> 7, (levels, lanes))
                lefts.append(jnp.where(along == along_index, 1.0, 0.0).astype(jnp.bfloat16))
                here = level == level_index
                tops, rests = [], []
                for c in range(4):
                    value = row(c)
                    top = value.astype(jnp.bfloat16).astype(jnp.float32)
                    rest = value - top
                    tops.append(jnp.where(here, jnp.broadcast_to(top, (levels, lanes)), 0.0).astype(jnp.bfloat16))
                    rests.append(jnp.where(here, jnp.broadcast_to(rest, (levels, lanes)), 0.0).astype(jnp.bfloat16))
                rights.append(jnp.concatenate(tops + rests, axis=0))
        left = jnp.concatenate(lefts, axis=1)
        right = jnp.concatenate(rights, axis=1)
        acc_ref[...] += lax.dot_general(left, right, (((1,), (1,)), ((), ())), preferred_element_type=jnp.float32)
        return carry

    lax.fori_loop(0, sources // group, add, 0)
    half = 4 * levels
    sums = (acc_ref[:, :half] + acc_ref[:, half:]).T
    total = mass_ref[...] + sums[:levels]
    inverse = 1.0 / total
    fields = []
    for c in range(3):
        value = (momentum_ref[c * levels : (c + 1) * levels, :] + sums[(c + 1) * levels : (c + 2) * levels]) / total
        vel_ref[c * levels : (c + 1) * levels, :] = value
        field_ref[c * levels : (c + 1) * levels, :] = value
        fields.append(value)
    stiffness = 0.5 + inverse
    field_ref[3 * levels : 4 * levels, :] = stiffness
    fields.append(stiffness)
    turned = jnp.concatenate(fields, axis=0).T
    strip_ref[0:8, :] = turned[0:8]
    strip_ref[8:16, :] = turned[lanes - 8 : lanes]


def deposit(incoming, fluid_mass, fluid_momentum):
    levels, lanes = fluid_mass.shape
    return pl.pallas_call(
        deposit_kernel,
        out_shape=(
            jax.ShapeDtypeStruct((3 * levels, lanes), jnp.float32),
            jax.ShapeDtypeStruct((4 * levels, lanes), jnp.float32),
            jax.ShapeDtypeStruct((16, lanes), jnp.float32),
        ),
        scratch_shapes=[pltpu.VMEM((lanes, 8 * levels), jnp.float32)],
        name="deposit",
    )(incoming, fluid_mass, fluid_momentum)


def shifts(axes, sizes):
    gx, gy = sizes
    dx, dy = axes
    return [
        (x * gy + y, (x + dx) * gy + y + dy)
        for x in range(gx)
        for y in range(gy)
        if 0 <= x + dx < gx and 0 <= y + dy < gy
    ]


def solve_kernel(field_ref, below_ref, above_ref, left_ref, right_ref, bl_ref, br_ref, al_ref, ar_ref, out_ref):
    depth = 4
    lanes = out_ref.shape[1]
    levels = out_ref.shape[0]
    rim = WIDTH * depth
    zero = jnp.zeros((lanes - 16, lanes), jnp.float32)

    def sidewise(right, left):
        return jnp.concatenate([right, zero, left], axis=0).T

    lane = lax.broadcasted_iota(jnp.int32, (levels, lanes), 1)
    own_side = sidewise(right_ref[...], left_ref[...])
    below_side = sidewise(br_ref[...], bl_ref[...])
    above_side = sidewise(ar_ref[...], al_ref[...])
    wide = []
    near = (lax.broadcasted_iota(jnp.int32, (levels + 2 * rim, lanes), 1) < WIDTH) | (
        lax.broadcasted_iota(jnp.int32, (levels + 2 * rim, lanes), 1) >= lanes - WIDTH
    )
    for f in range(4):
        first = jnp.concatenate(
            [below_ref[f], field_ref[f * levels : (f + 1) * levels, :], above_ref[f]], axis=0
        )
        second = jnp.concatenate(
            [
                below_side[(f + 1) * levels - rim : (f + 1) * levels],
                own_side[f * levels : (f + 1) * levels],
                above_side[f * levels : f * levels + rim],
            ],
            axis=0,
        )
        wide.append(jnp.concatenate([first, jnp.where(near, second, 0.0)], axis=1))
    u, v, w, stiffness = wide
    total_rows = levels + 2 * rim

    def roll_rows(value, amount):
        return pltpu.roll(value, amount % total_rows, 0)

    def roll_lanes(value, amount):
        return pltpu.roll(value, amount % (2 * lanes), 1)

    row = lax.broadcasted_iota(jnp.int32, (total_rows, 2 * lanes), 0)
    z = row % depth

    def above_z(value):
        return jnp.where(z == depth - 1, 0.0, roll_rows(value, -1))

    def below_z(value):
        return jnp.where(z == 0, 0.0, roll_rows(value, 1))

    inside = stiffness > 0.0
    source = -0.5 * (
        (roll_rows(u, -depth) - roll_rows(u, depth))
        + (roll_lanes(v, -1) - roll_lanes(v, 1))
        + (above_z(w) - below_z(w))
    )
    source = jnp.where(inside, source, 0.0)
    theta = (eigen_high + eigen_low) / 2.0
    delta = (eigen_high - eigen_low) / 2.0
    sigma = theta / delta
    rho = 1.0 / sigma
    pressure = jnp.zeros_like(source)
    residual = source
    search = source / theta
    for sweep in range(SWEEPS):
        pressure = pressure + search
        if sweep + 1 < SWEEPS:
            beside = (
                roll_rows(search, -depth) + roll_rows(search, depth)
                + roll_lanes(search, -1) + roll_lanes(search, 1)
                + above_z(search) + below_z(search)
            )
            residual = residual - ((6.0 + stiffness) * search - beside)
            rho_new = 1.0 / (2.0 * sigma - rho)
            search = rho_new * rho * search + 2.0 * rho_new / delta * residual
            search = jnp.where(inside, search, 0.0)
            rho = rho_new
    out_ref[...] = pressure[rim : rim + levels, :lanes]


def local(destination, row_count, old_cell, new_cell, point_mass, point_vel, grid_delta, fluid_mass, fluid_momentum):
    rows, lanes = point_mass.shape
    across, depth, along = fluid_mass.shape
    levels = across * depth
    sizes = (lax.axis_size("gx"), lax.axis_size("gy"))
    owners = sizes[0] * sizes[1]
    outgoing = pack(
        destination.reshape(1, rows),
        row_count.reshape(1, rows),
        old_cell,
        new_cell,
        point_mass,
        jnp.swapaxes(point_vel, 0, 1),
        grid_delta.reshape(3 * levels, along),
    )
    incoming = lax.all_to_all(
        outgoing.reshape(owners, 1, CAP * FIELDS * lanes), ("gx", "gy"), split_axis=0, concat_axis=0, tiled=True
    ).reshape(owners * CAP * FIELDS, lanes)
    velocity, fields, strips = deposit(incoming, fluid_mass.reshape(levels, along), fluid_momentum.reshape(3 * levels, along))
    rim = WIDTH * depth
    both = ("gx", "gy")
    grouped = fields.reshape(4, levels, along)
    low_x, high_x = grouped[:, :rim], grouped[:, levels - rim :]
    low_y, high_y = strips[:8], strips[8:]

    def send(value, dx, dy):
        return lax.ppermute(value, both, shifts((dx, dy), sizes))

    below = send(high_x, 1, 0)
    above = send(low_x, -1, 0)
    left = send(high_y, 0, 1)
    right = send(low_y, 0, -1)
    below_left = send(high_y, 1, 1)
    below_right = send(low_y, 1, -1)
    above_left = send(high_y, -1, 1)
    above_right = send(low_y, -1, -1)
    pressure = pl.pallas_call(
        solve_kernel,
        out_shape=jax.ShapeDtypeStruct((levels, along), jnp.float32),
        name="solve",
    )(fields, below, above, left, right, below_left, below_right, above_left, above_right)
    return velocity.reshape(3, across, depth, along), pressure.reshape(across, depth, along)


def solution(mesh):
    return jax.shard_map(
        local,
        mesh=mesh,
        in_specs=(
            P(("gx", "gy"), None),
            P(("gx", "gy")),
            P(("gx", "gy"), None),
            P(("gx", "gy"), None),
            P(("gx", "gy"), None),
            P(("gx", "gy"), None, None),
            P(None, "gx", None, "gy"),
            P("gx", None, "gy"),
            P(None, "gx", None, "gy"),
        ),
        out_specs=(P(None, "gx", None, "gy"), P("gx", None, "gy")),
        check_vma=False,
    )
```

```python
import jax
import jax.numpy as jnp
from jax import lax
from jax.experimental import pallas as pl
from jax.experimental.pallas import tpu as pltpu
from jax.sharding import PartitionSpec as P

CAP = 3
FIELDS = 5
SWEEPS = 4
WIDTH = 4

eigen_low = 0.5
eigen_high = 14.5


def iota_bf(shape):
    return lax.broadcasted_iota(jnp.int32, shape, 0).astype(jnp.float32).astype(jnp.bfloat16)

def deposit_kernel(group, form, in_ref, mass_ref, momentum_ref, vel_ref, field_ref, low_ref, high_ref, down_ref, up_ref, acc_ref):
    lanes = in_ref.shape[1]
    levels = mass_ref.shape[0]
    sources = in_ref.shape[0] // (CAP * FIELDS)
    acc_ref[...] = jnp.zeros_like(acc_ref)
    along_index = iota_bf((lanes, lanes))
    level_index = iota_bf((levels, lanes))

    def add(index, carry):
        lefts, rights = [], []
        for g in range(group):
            base = (index * group + g) * (CAP * FIELDS)
            for s in range(CAP):
                row = lambda f: in_ref[pl.ds(base + f * CAP + s, 1), :]
                cell = row(4).astype(jnp.int32)
                along = jnp.broadcast_to((cell & (lanes - 1)).astype(jnp.float32), (lanes, lanes)).astype(jnp.bfloat16)
                level = jnp.broadcast_to((cell >> 7).astype(jnp.float32), (levels, lanes)).astype(jnp.bfloat16)
                lefts.append(jnp.where(along == along_index, jnp.ones((lanes, lanes), jnp.bfloat16), jnp.zeros((lanes, lanes), jnp.bfloat16)))
                here = level == level_index
                nothing = jnp.zeros((levels, lanes), jnp.bfloat16)
                tops, rests = [], []
                for c in range(4):
                    value = jnp.broadcast_to(row(c), (levels, lanes))
                    top = value.astype(jnp.bfloat16)
                    rest = (value - top.astype(jnp.float32)).astype(jnp.bfloat16)
                    tops.append(jnp.where(here, top, nothing))
                    rests.append(jnp.where(here, rest, nothing))
                rights.append(jnp.concatenate(tops + rests, axis=0))
        left = jnp.concatenate(lefts, axis=1)
        right = jnp.concatenate(rights, axis=1)
        if form == "NT":
            acc_ref[...] += lax.dot_general(left, right, (((1,), (1,)), ((), ())), preferred_element_type=jnp.float32)
        else:
            acc_ref[...] += lax.dot_general(right, left, (((1,), (1,)), ((), ())), preferred_element_type=jnp.float32)
        return carry

    lax.fori_loop(0, sources // group, add, 0)
    half = 4 * levels
    if form == "NT":
        sums = (acc_ref[:, :half] + acc_ref[:, half:]).T
    else:
        sums = acc_ref[:half, :] + acc_ref[half:, :]
    total = mass_ref[...] + sums[:levels]
    inverse = 1.0 / total
    fields = []
    for c in range(3):
        value = (momentum_ref[c * levels : (c + 1) * levels, :] + sums[(c + 1) * levels : (c + 2) * levels]) / total
        vel_ref[c * levels : (c + 1) * levels, :] = value
        field_ref[c * levels : (c + 1) * levels, :] = value
        fields.append(value)
    stiffness = 0.5 + inverse
    field_ref[3 * levels : 4 * levels, :] = stiffness
    fields.append(stiffness)
    turned = jnp.concatenate(fields, axis=0).T
    low_ref[...] = turned[0:8]
    high_ref[...] = turned[lanes - 8 : lanes]
    rim = down_ref.shape[1]
    for f in range(4):
        down_ref[f] = fields[f][:rim]
        up_ref[f] = fields[f][levels - rim :]

def deposit(incoming, fluid_mass, fluid_momentum, group=8, form="NTs", name="deposit", vmem=24<<20):
    levels, lanes = fluid_mass.shape
    return pl.pallas_call(
        functools.partial(deposit_kernel, group, form),
        out_shape=(
            jax.ShapeDtypeStruct((3 * levels, lanes), jnp.float32),
            jax.ShapeDtypeStruct((4 * levels, lanes), jnp.float32),
            jax.ShapeDtypeStruct((8, lanes), jnp.float32),
            jax.ShapeDtypeStruct((8, lanes), jnp.float32),
            jax.ShapeDtypeStruct((4, WIDTH * 4, lanes), jnp.float32),
            jax.ShapeDtypeStruct((4, WIDTH * 4, lanes), jnp.float32),
        ),
        scratch_shapes=[pltpu.VMEM((lanes, 8 * levels) if form == "NT" else (8 * levels, lanes), jnp.float32)],
        compiler_params=pltpu.CompilerParams(vmem_limit_bytes=vmem),
        name=name,
    )(incoming, fluid_mass, fluid_momentum)

def pieces(value):
    top = value.astype(jnp.bfloat16)
    rest = value - top.astype(jnp.float32)
    middle = rest.astype(jnp.bfloat16)
    return top, middle, (rest - middle.astype(jnp.float32)).astype(jnp.bfloat16)


def pack_kernel(*refs):
    inputs, out_ref, staged, (live_ref, pay_ref, sem) = refs[:7], refs[7], refs[8:15], refs[15:]
    copies = [pltpu.make_async_copy(src, dst, sem.at[i]) for i, (src, dst) in enumerate(zip(inputs, staged))]
    for copy in copies:
        copy.start()
    target_ref, count_ref, old_ref, new_ref, mass_ref, vel_ref, delta_ref = staged
    rows, lanes = mass_ref.shape
    owners = out_ref.shape[0] // (CAP * FIELDS)
    levels = delta_ref.shape[0] // 3
    copies[0].wait()
    target = jnp.broadcast_to(target_ref[...], (owners, rows))
    marks = target == lax.broadcasted_iota(jnp.int32, (owners, rows), 0)
    before = lax.broadcasted_iota(jnp.int32, (rows, rows), 0) < lax.broadcasted_iota(jnp.int32, (rows, rows), 1)
    ones = jnp.where(marks, 1.0, 0.0)
    earlier = jnp.dot(
        ones.astype(jnp.bfloat16), jnp.where(before, 1.0, 0.0).astype(jnp.bfloat16), preferred_element_type=jnp.float32
    )
    for copy in copies[1:]:
        copy.wait()
    lane_index = lax.broadcasted_iota(jnp.int32, (lanes, lanes), 1).astype(jnp.float32)
    for part in range(rows // lanes):
        band = slice(part * lanes, (part + 1) * lanes)
        counts = jnp.broadcast_to(count_ref[:, band].astype(jnp.float32), (lanes, lanes)).T
        live_ref[band, :] = jnp.where(lane_index < counts, mass_ref[band, :], 0.0)
    step = 16

    def gather(index, carry):
        band = pl.ds(pl.multiple_of(index * step, step), step)
        cell = old_ref[band, :]
        along = cell & (lanes - 1)
        level = cell >> 7
        found = [jnp.zeros((step, lanes), jnp.float32)] * 3
        for h in range(levels):
            mask = level == h
            for c in range(3):
                table = jnp.broadcast_to(delta_ref[c * levels + h : c * levels + h + 1, :], (step, lanes))
                found[c] = jnp.where(mask, jnp.take_along_axis(table, along, axis=1), found[c])
        mass = live_ref[band, :]
        parts = [mass] + [mass * (vel_ref[c, band, :] + found[c]) for c in range(3)]
        parts.append(new_ref[band, :].astype(jnp.float32))
        for f, part in enumerate(parts):
            for k, piece in enumerate(pieces(part)):
                pay_ref[pl.ds(pl.multiple_of(k * rows + index * step, step), step), f * lanes : (f + 1) * lanes] = piece
        return carry

    lax.fori_loop(0, rows // step, gather, 0)
    for s in range(CAP):
        chosen = jnp.where(earlier == float(s), ones, 0.0).astype(jnp.bfloat16)
        picked = jnp.dot(jnp.concatenate([chosen] * 3, axis=1), pay_ref[...], preferred_element_type=jnp.float32)
        for f in range(FIELDS):
            out_ref[pl.ds(f * CAP + s, owners, stride=CAP * FIELDS), :] = picked[:, f * lanes : (f + 1) * lanes]


def pack(*args):
    rows, lanes = args[4].shape
    owners = lax.axis_size("gx") * lax.axis_size("gy")
    return pl.pallas_call(
        pack_kernel,
        out_shape=jax.ShapeDtypeStruct((owners * CAP * FIELDS, lanes), jnp.float32),
        in_specs=[pl.BlockSpec(memory_space=pltpu.MemorySpace.HBM)] * len(args),
        scratch_shapes=[pltpu.VMEM(a.shape, a.dtype) for a in args]
        + [
            pltpu.VMEM((rows, lanes), jnp.float32),
            pltpu.VMEM((3 * rows, FIELDS * lanes), jnp.bfloat16),
            pltpu.SemaphoreType.DMA((len(args),)),
        ],
        compiler_params=pltpu.CompilerParams(vmem_limit_bytes=16 << 20),
        name="pack",
    )(*[pltpu.with_memory_space_constraint(a, pltpu.MemorySpace.HBM) for a in args])


def whole(shape, value):
    return jnp.full(shape, value, jnp.bfloat16)


def row_index(shape):
    return lax.broadcasted_iota(jnp.int32, shape, 0).astype(jnp.float32).astype(jnp.bfloat16)


def deposit_kernel(in_ref, mass_ref, momentum_ref, field_ref, low_ref, high_ref, down_ref, up_ref, acc_ref):
    lanes = in_ref.shape[1]
    levels = mass_ref.shape[0]
    sources = in_ref.shape[0] // (CAP * FIELDS)
    group = 32
    acc_ref[...] = jnp.zeros_like(acc_ref)
    along_index = row_index((lanes, lanes))
    level_index = row_index((levels, lanes))

    def add(index, carry):
        lefts, rights = [], []
        for g in range(group):
            base = (index * group + g) * (CAP * FIELDS)
            for s in range(CAP):
                row = lambda f: in_ref[pl.ds(base + f * CAP + s, 1), :]
                cell = row(4).astype(jnp.int32)
                along = jnp.broadcast_to((cell & (lanes - 1)).astype(jnp.float32), (lanes, lanes)).astype(jnp.bfloat16)
                level = jnp.broadcast_to((cell >> 7).astype(jnp.float32), (levels, lanes)).astype(jnp.bfloat16)
                lefts.append(jnp.where(along == along_index, whole((lanes, lanes), 1.0), whole((lanes, lanes), 0.0)))
                here = level == level_index
                nothing = whole((levels, lanes), 0.0)
                tops, rests = [], []
                for c in range(4):
                    value = jnp.broadcast_to(row(c), (levels, lanes))
                    top = value.astype(jnp.bfloat16)
                    rest = (value - top.astype(jnp.float32)).astype(jnp.bfloat16)
                    tops.append(jnp.where(here, top, nothing))
                    rests.append(jnp.where(here, rest, nothing))
                rights.append(jnp.concatenate(tops + rests, axis=0))
        left = jnp.concatenate(lefts, axis=1)
        right = jnp.concatenate(rights, axis=1)
        acc_ref[...] += lax.dot_general(right, left, (((1,), (1,)), ((), ())), preferred_element_type=jnp.float32)
        return carry

    lax.fori_loop(0, sources // group, add, 0)
    half = 4 * levels
    sums = acc_ref[:half, :] + acc_ref[half:, :]
    finish(sums, mass_ref, momentum_ref, field_ref, low_ref, high_ref, down_ref, up_ref)


def finish(sums, mass_ref, momentum_ref, field_ref, low_ref, high_ref, down_ref, up_ref):
    levels, lanes = mass_ref.shape
    total = mass_ref[...] + sums[:levels]
    fields = [
        (momentum_ref[c * levels : (c + 1) * levels, :] + sums[(c + 1) * levels : (c + 2) * levels]) / total
        for c in range(3)
    ]
    fields.append(0.5 + 1.0 / total)
    rim = down_ref.shape[1]
    for f, field in enumerate(fields):
        field_ref[f * levels : (f + 1) * levels, :] = field
        down_ref[f] = field[:rim]
        up_ref[f] = field[levels - rim :]
    turned = jnp.concatenate(fields, axis=0).T
    low_ref[...] = turned[0:8]
    high_ref[...] = turned[lanes - 8 : lanes]


def deposit(incoming, fluid_mass, fluid_momentum):
    levels, lanes = fluid_mass.shape
    shapes = [(4 * levels, lanes), (8, lanes), (8, lanes), (4, WIDTH * 4, lanes), (4, WIDTH * 4, lanes)]
    return pl.pallas_call(
        deposit_kernel,
        out_shape=tuple(jax.ShapeDtypeStruct(shape, jnp.float32) for shape in shapes),
        scratch_shapes=[pltpu.VMEM((8 * levels, lanes), jnp.float32)],
        compiler_params=pltpu.CompilerParams(vmem_limit_bytes=24 << 20),
        name="deposit",
    )(incoming, fluid_mass, fluid_momentum)


def shifts(axes, sizes):
    gx, gy = sizes
    dx, dy = axes
    return [
        (x * gy + y, (x + dx) * gy + y + dy)
        for x in range(gx)
        for y in range(gy)
        if 0 <= x + dx < gx and 0 <= y + dy < gy
    ]


def solve_kernel(field_ref, left_ref, right_ref, below_ref, above_ref, vel_ref, out_ref, sem):
    copy = pltpu.make_async_copy(field_ref.at[: vel_ref.shape[0]], vel_ref, sem)
    copy.start()
    depth = 4
    lanes = out_ref.shape[1]
    levels = out_ref.shape[0]
    rim = WIDTH * depth
    faces = 4 * rim
    zero = jnp.zeros((lanes - 16, lanes), jnp.float32)

    def sidewise(right, left):
        return jnp.concatenate([right, zero, left], axis=0).T

    own_side = sidewise(right_ref[...], left_ref[...])
    below_side = sidewise(below_ref[faces + 8 :], below_ref[faces : faces + 8])
    above_side = sidewise(above_ref[faces + 8 :], above_ref[faces : faces + 8])
    wide = []
    near = (lax.broadcasted_iota(jnp.int32, (levels + 2 * rim, lanes), 1) < WIDTH) | (
        lax.broadcasted_iota(jnp.int32, (levels + 2 * rim, lanes), 1) >= lanes - WIDTH
    )
    for f in range(4):
        first = jnp.concatenate(
            [below_ref[f * rim : (f + 1) * rim], field_ref[f * levels : (f + 1) * levels, :], above_ref[f * rim : (f + 1) * rim]], axis=0
        )
        second = jnp.concatenate(
            [
                below_side[(f + 1) * levels - rim : (f + 1) * levels],
                own_side[f * levels : (f + 1) * levels],
                above_side[f * levels : f * levels + rim],
            ],
            axis=0,
        )
        wide.append(jnp.concatenate([first, jnp.where(near, second, 0.0)], axis=1))
    u, v, w, stiffness = wide
    total_rows = levels + 2 * rim

    def roll_rows(value, amount):
        return pltpu.roll(value, amount % total_rows, 0)

    def roll_lanes(value, amount):
        return pltpu.roll(value, amount % (2 * lanes), 1)

    row = lax.broadcasted_iota(jnp.int32, (total_rows, 2 * lanes), 0)
    z = row % depth

    def above_z(value):
        return jnp.where(z == depth - 1, 0.0, roll_rows(value, -1))

    def below_z(value):
        return jnp.where(z == 0, 0.0, roll_rows(value, 1))

    inside = stiffness > 0.0
    source = -0.5 * (
        (roll_rows(u, -depth) - roll_rows(u, depth))
        + (roll_lanes(v, -1) - roll_lanes(v, 1))
        + (above_z(w) - below_z(w))
    )
    source = jnp.where(inside, source, 0.0)
    theta = (eigen_high + eigen_low) / 2.0
    delta = (eigen_high - eigen_low) / 2.0
    sigma = theta / delta
    rho = 1.0 / sigma
    pressure = jnp.zeros_like(source)
    residual = source
    search = source / theta
    for sweep in range(SWEEPS):
        pressure = pressure + search
        if sweep + 1 < SWEEPS:
            beside = (
                roll_rows(search, -depth) + roll_rows(search, depth)
                + roll_lanes(search, -1) + roll_lanes(search, 1)
                + above_z(search) + below_z(search)
            )
            residual = residual - ((6.0 + stiffness) * search - beside)
            rho_new = 1.0 / (2.0 * sigma - rho)
            search = rho_new * rho * search + 2.0 * rho_new / delta * residual
            search = jnp.where(inside, search, 0.0)
            rho = rho_new
    out_ref[...] = pressure[rim : rim + levels, :lanes]
    copy.wait()


def local(destination, row_count, old_cell, new_cell, point_mass, point_vel, grid_delta, fluid_mass, fluid_momentum):
    rows, lanes = point_mass.shape
    across, depth, along = fluid_mass.shape
    levels = across * depth
    sizes = (lax.axis_size("gx"), lax.axis_size("gy"))
    owners = sizes[0] * sizes[1]
    outgoing = pack(
        destination.reshape(1, rows),
        row_count.reshape(1, rows),
        old_cell,
        new_cell,
        point_mass,
        jnp.swapaxes(point_vel, 0, 1),
        grid_delta.reshape(3 * levels, along),
    )
    incoming = lax.all_to_all(
        outgoing.reshape(owners, 1, CAP * FIELDS * lanes), ("gx", "gy"), split_axis=0, concat_axis=0, tiled=True
    ).reshape(owners * CAP * FIELDS, lanes)
    fields, low_y, high_y, low_x, high_x = deposit(
        incoming, fluid_mass.reshape(levels, along), fluid_momentum.reshape(3 * levels, along)
    )

    def send(value, dx, dy):
        return lax.ppermute(value, ("gx", "gy"), shifts((dx, dy), sizes))

    left = send(high_y, 0, 1)
    right = send(low_y, 0, -1)
    faces = 4 * WIDTH * depth
    below = send(jnp.concatenate([high_x.reshape(faces, along), left, right], axis=0), 1, 0)
    above = send(jnp.concatenate([low_x.reshape(faces, along), left, right], axis=0), -1, 0)
    velocity, pressure = pl.pallas_call(
        solve_kernel,
        out_shape=(
            jax.ShapeDtypeStruct((3 * levels, along), jnp.float32),
            jax.ShapeDtypeStruct((levels, along), jnp.float32),
        ),
        out_specs=(pl.BlockSpec(memory_space=pltpu.MemorySpace.HBM), pl.BlockSpec(memory_space=pltpu.MemorySpace.VMEM)),
        scratch_shapes=[pltpu.SemaphoreType.DMA],
        compiler_params=pltpu.CompilerParams(vmem_limit_bytes=8 << 20),
        name="solve",
    )(fields, left, right, below, above)
    return velocity.reshape(3, across, depth, along), pressure.reshape(across, depth, along)


def solution(mesh):
    return jax.shard_map(
        local,
        mesh=mesh,
        in_specs=(
            P(("gx", "gy"), None),
            P(("gx", "gy")),
            P(("gx", "gy"), None),
            P(("gx", "gy"), None),
            P(("gx", "gy"), None),
            P(("gx", "gy"), None, None),
            P(None, "gx", None, "gy"),
            P("gx", None, "gy"),
            P(None, "gx", None, "gy"),
        ),
        out_specs=(P(None, "gx", None, "gy"), P("gx", None, "gy")),
        check_vma=False,
    )
```

```python
import functools

import jax
import jax.numpy as jnp
from jax import lax
from jax.experimental import pallas as pl
from jax.experimental.pallas import tpu as pltpu
from jax.sharding import PartitionSpec as P

CAP = 3
FIELDS = 5
SWEEPS = 4
WIDTH = 4

eigen_low = 0.5
eigen_high = 14.5


def iota_bf(shape):
    return lax.broadcasted_iota(jnp.int32, shape, 0).astype(jnp.float32).astype(jnp.bfloat16)

def deposit_kernel(group, form, in_ref, mass_ref, momentum_ref, vel_ref, field_ref, low_ref, high_ref, down_ref, up_ref, acc_ref):
    lanes = in_ref.shape[1]
    levels = mass_ref.shape[0]
    sources = in_ref.shape[0] // (CAP * FIELDS)
    acc_ref[...] = jnp.zeros_like(acc_ref)
    along_index = iota_bf((lanes, lanes))
    level_index = iota_bf((levels, lanes))

    def add(index, carry):
        lefts, rights = [], []
        for g in range(group):
            base = (index * group + g) * (CAP * FIELDS)
            for s in range(CAP):
                row = lambda f: in_ref[pl.ds(base + f * CAP + s, 1), :]
                cell = row(4).astype(jnp.int32)
                along = jnp.broadcast_to((cell & (lanes - 1)).astype(jnp.float32), (lanes, lanes)).astype(jnp.bfloat16)
                level = jnp.broadcast_to((cell >> 7).astype(jnp.float32), (levels, lanes)).astype(jnp.bfloat16)
                lefts.append(jnp.where(along == along_index, jnp.ones((lanes, lanes), jnp.bfloat16), jnp.zeros((lanes, lanes), jnp.bfloat16)))
                here = level == level_index
                nothing = jnp.zeros((levels, lanes), jnp.bfloat16)
                tops, rests = [], []
                for c in range(4):
                    value = jnp.broadcast_to(row(c), (levels, lanes))
                    top = value.astype(jnp.bfloat16)
                    rest = (value - top.astype(jnp.float32)).astype(jnp.bfloat16)
                    tops.append(jnp.where(here, top, nothing))
                    rests.append(jnp.where(here, rest, nothing))
                rights.append(jnp.concatenate(tops + rests, axis=0))
        left = jnp.concatenate(lefts, axis=1)
        right = jnp.concatenate(rights, axis=1)
        if form == "NT":
            acc_ref[...] += lax.dot_general(left, right, (((1,), (1,)), ((), ())), preferred_element_type=jnp.float32)
        else:
            acc_ref[...] += lax.dot_general(right, left, (((1,), (1,)), ((), ())), preferred_element_type=jnp.float32)
        return carry

    lax.fori_loop(0, sources // group, add, 0)
    half = 4 * levels
    if form == "NT":
        sums = (acc_ref[:, :half] + acc_ref[:, half:]).T
    else:
        sums = acc_ref[:half, :] + acc_ref[half:, :]
    total = mass_ref[...] + sums[:levels]
    inverse = 1.0 / total
    fields = []
    for c in range(3):
        value = (momentum_ref[c * levels : (c + 1) * levels, :] + sums[(c + 1) * levels : (c + 2) * levels]) / total
        vel_ref[c * levels : (c + 1) * levels, :] = value
        field_ref[c * levels : (c + 1) * levels, :] = value
        fields.append(value)
    stiffness = 0.5 + inverse
    field_ref[3 * levels : 4 * levels, :] = stiffness
    fields.append(stiffness)
    turned = jnp.concatenate(fields, axis=0).T
    low_ref[...] = turned[0:8]
    high_ref[...] = turned[lanes - 8 : lanes]
    rim = down_ref.shape[1]
    for f in range(4):
        down_ref[f] = fields[f][:rim]
        up_ref[f] = fields[f][levels - rim :]

def deposit(incoming, fluid_mass, fluid_momentum, group=8, form="NTs", name="deposit", vmem=24<<20):
    levels, lanes = fluid_mass.shape
    return pl.pallas_call(
        functools.partial(deposit_kernel, group, form),
        out_shape=(
            jax.ShapeDtypeStruct((3 * levels, lanes), jnp.float32),
            jax.ShapeDtypeStruct((4 * levels, lanes), jnp.float32),
            jax.ShapeDtypeStruct((8, lanes), jnp.float32),
            jax.ShapeDtypeStruct((8, lanes), jnp.float32),
            jax.ShapeDtypeStruct((4, WIDTH * 4, lanes), jnp.float32),
            jax.ShapeDtypeStruct((4, WIDTH * 4, lanes), jnp.float32),
        ),
        scratch_shapes=[pltpu.VMEM((lanes, 8 * levels) if form == "NT" else (8 * levels, lanes), jnp.float32)],
        compiler_params=pltpu.CompilerParams(vmem_limit_bytes=vmem),
        name=name,
    )(incoming, fluid_mass, fluid_momentum)

def pieces(value):
    top = value.astype(jnp.bfloat16)
    rest = value - top.astype(jnp.float32)
    middle = rest.astype(jnp.bfloat16)
    return top, middle, (rest - middle.astype(jnp.float32)).astype(jnp.bfloat16)


def pack_kernel(*refs):
    inputs, out_ref, staged, (live_ref, pay_ref, sem) = refs[:7], refs[7], refs[8:15], refs[15:]
    copies = [pltpu.make_async_copy(src, dst, sem.at[i]) for i, (src, dst) in enumerate(zip(inputs, staged))]
    for copy in copies:
        copy.start()
    target_ref, count_ref, old_ref, new_ref, mass_ref, vel_ref, delta_ref = staged
    rows, lanes = mass_ref.shape
    owners = out_ref.shape[0] // (CAP * FIELDS)
    levels = delta_ref.shape[0] // 3
    copies[0].wait()
    target = jnp.broadcast_to(target_ref[...], (owners, rows))
    marks = target == lax.broadcasted_iota(jnp.int32, (owners, rows), 0)
    before = lax.broadcasted_iota(jnp.int32, (rows, rows), 0) < lax.broadcasted_iota(jnp.int32, (rows, rows), 1)
    ones = jnp.where(marks, 1.0, 0.0)
    earlier = jnp.dot(
        ones.astype(jnp.bfloat16), jnp.where(before, 1.0, 0.0).astype(jnp.bfloat16), preferred_element_type=jnp.float32
    )
    for copy in copies[1:]:
        copy.wait()
    lane_index = lax.broadcasted_iota(jnp.int32, (lanes, lanes), 1).astype(jnp.float32)
    for part in range(rows // lanes):
        band = slice(part * lanes, (part + 1) * lanes)
        counts = jnp.broadcast_to(count_ref[:, band].astype(jnp.float32), (lanes, lanes)).T
        live_ref[band, :] = jnp.where(lane_index < counts, mass_ref[band, :], 0.0)
    step = 16

    def gather(index, carry):
        band = pl.ds(pl.multiple_of(index * step, step), step)
        cell = old_ref[band, :]
        along = cell & (lanes - 1)
        level = cell >> 7
        found = [jnp.zeros((step, lanes), jnp.float32)] * 3
        for h in range(levels):
            mask = level == h
            for c in range(3):
                table = jnp.broadcast_to(delta_ref[c * levels + h : c * levels + h + 1, :], (step, lanes))
                found[c] = jnp.where(mask, jnp.take_along_axis(table, along, axis=1), found[c])
        mass = live_ref[band, :]
        parts = [mass] + [mass * (vel_ref[c, band, :] + found[c]) for c in range(3)]
        parts.append(new_ref[band, :].astype(jnp.float32))
        for f, part in enumerate(parts):
            for k, piece in enumerate(pieces(part)):
                pay_ref[pl.ds(pl.multiple_of(k * rows + index * step, step), step), f * lanes : (f + 1) * lanes] = piece
        return carry

    lax.fori_loop(0, rows // step, gather, 0)
    for s in range(CAP):
        chosen = jnp.where(earlier == float(s), ones, 0.0).astype(jnp.bfloat16)
        picked = jnp.dot(jnp.concatenate([chosen] * 3, axis=1), pay_ref[...], preferred_element_type=jnp.float32)
        for f in range(FIELDS):
            out_ref[pl.ds(f * CAP + s, owners, stride=CAP * FIELDS), :] = picked[:, f * lanes : (f + 1) * lanes]


def pack(*args):
    rows, lanes = args[4].shape
    owners = lax.axis_size("gx") * lax.axis_size("gy")
    return pl.pallas_call(
        pack_kernel,
        out_shape=jax.ShapeDtypeStruct((owners * CAP * FIELDS, lanes), jnp.float32),
        in_specs=[pl.BlockSpec(memory_space=pltpu.MemorySpace.HBM)] * len(args),
        scratch_shapes=[pltpu.VMEM(a.shape, a.dtype) for a in args]
        + [
            pltpu.VMEM((rows, lanes), jnp.float32),
            pltpu.VMEM((3 * rows, FIELDS * lanes), jnp.bfloat16),
            pltpu.SemaphoreType.DMA((len(args),)),
        ],
        compiler_params=pltpu.CompilerParams(vmem_limit_bytes=16 << 20),
        name="pack",
    )(*[pltpu.with_memory_space_constraint(a, pltpu.MemorySpace.HBM) for a in args])


def whole(shape, value):
    return jnp.full(shape, value, jnp.bfloat16)


def row_index(shape):
    return lax.broadcasted_iota(jnp.int32, shape, 0).astype(jnp.float32).astype(jnp.bfloat16)


def deposit_kernel(place_ref, in_ref, mass_ref, momentum_ref, field_ref, *rest):
    acc_ref = rest[-1]
    lanes = in_ref.shape[1]
    levels = mass_ref.shape[0]
    sources = in_ref.shape[0] // (CAP * FIELDS)
    group = 32
    acc_ref[...] = jnp.zeros_like(acc_ref)
    along_index = row_index((lanes, lanes))
    level_index = row_index((levels, lanes))

    def add(index, carry):
        lefts, rights = [], []
        for g in range(group):
            base = (index * group + g) * (CAP * FIELDS)
            for s in range(CAP):
                row = lambda f: in_ref[pl.ds(base + f * CAP + s, 1), :]
                cell = row(4).astype(jnp.int32)
                along = jnp.broadcast_to((cell & (lanes - 1)).astype(jnp.float32), (lanes, lanes)).astype(jnp.bfloat16)
                level = jnp.broadcast_to((cell >> 7).astype(jnp.float32), (levels, lanes)).astype(jnp.bfloat16)
                lefts.append(jnp.where(along == along_index, whole((lanes, lanes), 1.0), whole((lanes, lanes), 0.0)))
                here = level == level_index
                nothing = whole((levels, lanes), 0.0)
                tops, rests = [], []
                for c in range(4):
                    value = jnp.broadcast_to(row(c), (levels, lanes))
                    top = value.astype(jnp.bfloat16)
                    rest = (value - top.astype(jnp.float32)).astype(jnp.bfloat16)
                    tops.append(jnp.where(here, top, nothing))
                    rests.append(jnp.where(here, rest, nothing))
                rights.append(jnp.concatenate(tops + rests, axis=0))
        left = jnp.concatenate(lefts, axis=1)
        right = jnp.concatenate(rights, axis=1)
        acc_ref[...] += lax.dot_general(right, left, (((1,), (1,)), ((), ())), preferred_element_type=jnp.float32)
        return carry

    lax.fori_loop(0, sources // group, add, 0)
    half = 4 * levels
    sums = acc_ref[:half, :] + acc_ref[half:, :]
    finish(sums, place_ref, mass_ref, momentum_ref, field_ref, *rest[:-1])


def finish(sums, place_ref, mass_ref, momentum_ref, field_ref, inner_y_ref, outer_y_ref, inner_x_ref, outer_x_ref):
    levels, lanes = mass_ref.shape
    total = mass_ref[...] + sums[:levels]
    fields = [
        (momentum_ref[c * levels : (c + 1) * levels, :] + sums[(c + 1) * levels : (c + 2) * levels]) / total
        for c in range(3)
    ]
    fields.append(0.5 + 1.0 / total)
    rim = inner_x_ref.shape[0] // 4
    even_x = place_ref[0] % 2 == 0
    even_y = place_ref[1] % 2 == 0
    for f, field in enumerate(fields):
        field_ref[f * levels : (f + 1) * levels, :] = field
        low, high = field[:rim], field[levels - rim :]
        inner_x_ref[f * rim : (f + 1) * rim, :] = jnp.where(even_x, high, low)
        outer_x_ref[f * rim : (f + 1) * rim, :] = jnp.where(even_x, low, high)
    turned = jnp.concatenate(fields, axis=0).T
    low, high = turned[0:8], turned[lanes - 8 : lanes]
    inner_y_ref[...] = jnp.where(even_y, high, low)
    outer_y_ref[...] = jnp.where(even_y, low, high)


def deposit(place, incoming, fluid_mass, fluid_momentum):
    levels, lanes = fluid_mass.shape
    shapes = [(4 * levels, lanes), (8, lanes), (8, lanes), (4 * WIDTH * 4, lanes), (4 * WIDTH * 4, lanes)]
    vmem = pl.BlockSpec(memory_space=pltpu.MemorySpace.VMEM)
    return pl.pallas_call(
        deposit_kernel,
        out_shape=tuple(jax.ShapeDtypeStruct(shape, jnp.float32) for shape in shapes),
        in_specs=[pl.BlockSpec(memory_space=pltpu.MemorySpace.SMEM)] + [vmem] * 3,
        scratch_shapes=[pltpu.VMEM((8 * levels, lanes), jnp.float32)],
        compiler_params=pltpu.CompilerParams(vmem_limit_bytes=24 << 20),
        name="deposit",
    )(place, incoming, fluid_mass, fluid_momentum)


def swaps(axis, outer, sizes):
    pairs = []
    for x in range(sizes[0]):
        for y in range(sizes[1]):
            here = [x, y]
            forward = (here[axis] % 2 == 0) != outer
            here[axis] = (here[axis] + (1 if forward else -1)) % sizes[axis]
            pairs.append((x * sizes[1] + y, here[0] * sizes[1] + here[1]))
    return pairs


def solve_kernel(sizes, place_ref, field_ref, inner_y_ref, outer_y_ref, inner_x_ref, outer_x_ref, vel_ref, out_ref, sem):
    copy = pltpu.make_async_copy(field_ref.at[: vel_ref.shape[0]], vel_ref, sem)
    copy.start()
    depth = 4
    lanes = out_ref.shape[1]
    levels = out_ref.shape[0]
    rim = WIDTH * depth
    faces = 4 * rim
    zero = jnp.zeros((lanes - 16, lanes), jnp.float32)

    x, y = place_ref[0], place_ref[1]
    even_x, even_y = x % 2 == 0, y % 2 == 0
    has_below, has_above = x > 0, x < sizes[0] - 1
    has_left, has_right = y > 0, y < sizes[1] - 1

    def sidewise(inner, outer):
        right = jnp.where(has_right, jnp.where(even_y, inner, outer), 0.0)
        left = jnp.where(has_left, jnp.where(even_y, outer, inner), 0.0)
        return jnp.concatenate([right, zero, left], axis=0).T

    inner_x, outer_x = inner_x_ref[...], outer_x_ref[...]
    below = jnp.where(has_below, jnp.where(even_x, outer_x, inner_x), 0.0)
    above = jnp.where(has_above, jnp.where(even_x, inner_x, outer_x), 0.0)
    own_side = sidewise(inner_y_ref[...], outer_y_ref[...])
    below_side = sidewise(below[faces : faces + 8], below[faces + 8 :])
    above_side = sidewise(above[faces : faces + 8], above[faces + 8 :])
    wide = []
    near = (lax.broadcasted_iota(jnp.int32, (levels + 2 * rim, lanes), 1) < WIDTH) | (
        lax.broadcasted_iota(jnp.int32, (levels + 2 * rim, lanes), 1) >= lanes - WIDTH
    )
    for f in range(4):
        first = jnp.concatenate(
            [below[f * rim : (f + 1) * rim], field_ref[f * levels : (f + 1) * levels, :], above[f * rim : (f + 1) * rim]], axis=0
        )
        second = jnp.concatenate(
            [
                below_side[(f + 1) * levels - rim : (f + 1) * levels],
                own_side[f * levels : (f + 1) * levels],
                above_side[f * levels : f * levels + rim],
            ],
            axis=0,
        )
        wide.append(jnp.concatenate([first, jnp.where(near, second, 0.0)], axis=1))
    u, v, w, stiffness = wide
    total_rows = levels + 2 * rim

    def roll_rows(value, amount):
        return pltpu.roll(value, amount % total_rows, 0)

    def roll_lanes(value, amount):
        return pltpu.roll(value, amount % (2 * lanes), 1)

    row = lax.broadcasted_iota(jnp.int32, (total_rows, 2 * lanes), 0)
    z = row % depth

    def above_z(value):
        return jnp.where(z == depth - 1, 0.0, roll_rows(value, -1))

    def below_z(value):
        return jnp.where(z == 0, 0.0, roll_rows(value, 1))

    inside = stiffness > 0.0
    source = -0.5 * (
        (roll_rows(u, -depth) - roll_rows(u, depth))
        + (roll_lanes(v, -1) - roll_lanes(v, 1))
        + (above_z(w) - below_z(w))
    )
    source = jnp.where(inside, source, 0.0)
    theta = (eigen_high + eigen_low) / 2.0
    delta = (eigen_high - eigen_low) / 2.0
    sigma = theta / delta
    rho = 1.0 / sigma
    pressure = jnp.zeros_like(source)
    residual = source
    search = source / theta
    for sweep in range(SWEEPS):
        pressure = pressure + search
        if sweep + 1 < SWEEPS:
            beside = (
                roll_rows(search, -depth) + roll_rows(search, depth)
                + roll_lanes(search, -1) + roll_lanes(search, 1)
                + above_z(search) + below_z(search)
            )
            residual = residual - ((6.0 + stiffness) * search - beside)
            rho_new = 1.0 / (2.0 * sigma - rho)
            search = rho_new * rho * search + 2.0 * rho_new / delta * residual
            search = jnp.where(inside, search, 0.0)
            rho = rho_new
    out_ref[...] = pressure[rim : rim + levels, :lanes]
    copy.wait()


def local(destination, row_count, old_cell, new_cell, point_mass, point_vel, grid_delta, fluid_mass, fluid_momentum):
    rows, lanes = point_mass.shape
    across, depth, along = fluid_mass.shape
    levels = across * depth
    sizes = (lax.axis_size("gx"), lax.axis_size("gy"))
    owners = sizes[0] * sizes[1]
    place = jnp.stack([lax.axis_index("gx"), lax.axis_index("gy")]).astype(jnp.int32)
    place, destination = lax.optimization_barrier((place, destination))
    outgoing = pack(
        destination.reshape(1, rows),
        row_count.reshape(1, rows),
        old_cell,
        new_cell,
        point_mass,
        jnp.swapaxes(point_vel, 0, 1),
        grid_delta.reshape(3 * levels, along),
    )
    incoming = lax.all_to_all(
        outgoing.reshape(owners, 1, CAP * FIELDS * lanes), ("gx", "gy"), split_axis=0, concat_axis=0, tiled=True
    ).reshape(owners * CAP * FIELDS, lanes)
    fields, inner_y, outer_y, inner_x, outer_x = deposit(
        place, incoming, fluid_mass.reshape(levels, along), fluid_momentum.reshape(3 * levels, along)
    )

    def swap(value, axis, outer):
        return lax.ppermute(value, ("gx", "gy"), swaps(axis, outer, sizes))

    inner_y = swap(inner_y, 1, False)
    outer_y = swap(outer_y, 1, True)
    inner_x = swap(jnp.concatenate([inner_x, inner_y, outer_y], axis=0), 0, False)
    outer_x = swap(jnp.concatenate([outer_x, inner_y, outer_y], axis=0), 0, True)
    vmem = pl.BlockSpec(memory_space=pltpu.MemorySpace.VMEM)
    velocity, pressure = pl.pallas_call(
        functools.partial(solve_kernel, sizes),
        out_shape=(
            jax.ShapeDtypeStruct((3 * levels, along), jnp.float32),
            jax.ShapeDtypeStruct((levels, along), jnp.float32),
        ),
        in_specs=[pl.BlockSpec(memory_space=pltpu.MemorySpace.SMEM)] + [vmem] * 5,
        out_specs=(pl.BlockSpec(memory_space=pltpu.MemorySpace.HBM), vmem),
        scratch_shapes=[pltpu.SemaphoreType.DMA],
        compiler_params=pltpu.CompilerParams(vmem_limit_bytes=8 << 20),
        name="solve",
    )(place, fields, inner_y, outer_y, inner_x, outer_x)
    return velocity.reshape(3, across, depth, along), pressure.reshape(across, depth, along)


def solution(mesh):
    return jax.shard_map(
        local,
        mesh=mesh,
        in_specs=(
            P(("gx", "gy"), None),
            P(("gx", "gy")),
            P(("gx", "gy"), None),
            P(("gx", "gy"), None),
            P(("gx", "gy"), None),
            P(("gx", "gy"), None, None),
            P(None, "gx", None, "gy"),
            P("gx", None, "gy"),
            P(None, "gx", None, "gy"),
        ),
        out_specs=(P(None, "gx", None, "gy"), P("gx", None, "gy")),
        check_vma=False,
    )
```

```python
import functools

import jax
import jax.numpy as jnp
from jax import lax
from jax.experimental import pallas as pl
from jax.experimental.pallas import tpu as pltpu
from jax.sharding import PartitionSpec as P

CAP = 3
FIELDS = 5
SWEEPS = 4
WIDTH = 4

eigen_low = 0.5
eigen_high = 14.5


def iota_bf(shape):
    return lax.broadcasted_iota(jnp.int32, shape, 0).astype(jnp.float32).astype(jnp.bfloat16)

def deposit_kernel(group, form, in_ref, mass_ref, momentum_ref, vel_ref, field_ref, low_ref, high_ref, down_ref, up_ref, acc_ref):
    lanes = in_ref.shape[1]
    levels = mass_ref.shape[0]
    sources = in_ref.shape[0] // (CAP * FIELDS)
    acc_ref[...] = jnp.zeros_like(acc_ref)
    along_index = iota_bf((lanes, lanes))
    level_index = iota_bf((levels, lanes))

    def add(index, carry):
        lefts, rights = [], []
        for g in range(group):
            base = (index * group + g) * (CAP * FIELDS)
            for s in range(CAP):
                row = lambda f: in_ref[pl.ds(base + f * CAP + s, 1), :]
                cell = row(4).astype(jnp.int32)
                along = jnp.broadcast_to((cell & (lanes - 1)).astype(jnp.float32), (lanes, lanes)).astype(jnp.bfloat16)
                level = jnp.broadcast_to((cell >> 7).astype(jnp.float32), (levels, lanes)).astype(jnp.bfloat16)
                lefts.append(jnp.where(along == along_index, jnp.ones((lanes, lanes), jnp.bfloat16), jnp.zeros((lanes, lanes), jnp.bfloat16)))
                here = level == level_index
                nothing = jnp.zeros((levels, lanes), jnp.bfloat16)
                tops, rests = [], []
                for c in range(4):
                    value = jnp.broadcast_to(row(c), (levels, lanes))
                    top = value.astype(jnp.bfloat16)
                    rest = (value - top.astype(jnp.float32)).astype(jnp.bfloat16)
                    tops.append(jnp.where(here, top, nothing))
                    rests.append(jnp.where(here, rest, nothing))
                rights.append(jnp.concatenate(tops + rests, axis=0))
        left = jnp.concatenate(lefts, axis=1)
        right = jnp.concatenate(rights, axis=1)
        if form == "NT":
            acc_ref[...] += lax.dot_general(left, right, (((1,), (1,)), ((), ())), preferred_element_type=jnp.float32)
        else:
            acc_ref[...] += lax.dot_general(right, left, (((1,), (1,)), ((), ())), preferred_element_type=jnp.float32)
        return carry

    lax.fori_loop(0, sources // group, add, 0)
    half = 4 * levels
    if form == "NT":
        sums = (acc_ref[:, :half] + acc_ref[:, half:]).T
    else:
        sums = acc_ref[:half, :] + acc_ref[half:, :]
    total = mass_ref[...] + sums[:levels]
    inverse = 1.0 / total
    fields = []
    for c in range(3):
        value = (momentum_ref[c * levels : (c + 1) * levels, :] + sums[(c + 1) * levels : (c + 2) * levels]) / total
        vel_ref[c * levels : (c + 1) * levels, :] = value
        field_ref[c * levels : (c + 1) * levels, :] = value
        fields.append(value)
    stiffness = 0.5 + inverse
    field_ref[3 * levels : 4 * levels, :] = stiffness
    fields.append(stiffness)
    turned = jnp.concatenate(fields, axis=0).T
    low_ref[...] = turned[0:8]
    high_ref[...] = turned[lanes - 8 : lanes]
    rim = down_ref.shape[1]
    for f in range(4):
        down_ref[f] = fields[f][:rim]
        up_ref[f] = fields[f][levels - rim :]

def deposit(incoming, fluid_mass, fluid_momentum, group=8, form="NTs", name="deposit", vmem=24<<20):
    levels, lanes = fluid_mass.shape
    return pl.pallas_call(
        functools.partial(deposit_kernel, group, form),
        out_shape=(
            jax.ShapeDtypeStruct((3 * levels, lanes), jnp.float32),
            jax.ShapeDtypeStruct((4 * levels, lanes), jnp.float32),
            jax.ShapeDtypeStruct((8, lanes), jnp.float32),
            jax.ShapeDtypeStruct((8, lanes), jnp.float32),
            jax.ShapeDtypeStruct((4, WIDTH * 4, lanes), jnp.float32),
            jax.ShapeDtypeStruct((4, WIDTH * 4, lanes), jnp.float32),
        ),
        scratch_shapes=[pltpu.VMEM((lanes, 8 * levels) if form == "NT" else (8 * levels, lanes), jnp.float32)],
        compiler_params=pltpu.CompilerParams(vmem_limit_bytes=vmem),
        name=name,
    )(incoming, fluid_mass, fluid_momentum)

def pieces(value):
    top = value.astype(jnp.bfloat16)
    rest = value - top.astype(jnp.float32)
    middle = rest.astype(jnp.bfloat16)
    return top, middle, (rest - middle.astype(jnp.float32)).astype(jnp.bfloat16)


def pack_kernel(*refs):
    inputs, out_ref, staged, (live_ref, pay_ref, sem) = refs[:7], refs[7], refs[8:15], refs[15:]
    copies = [pltpu.make_async_copy(src, dst, sem.at[i]) for i, (src, dst) in enumerate(zip(inputs, staged))]
    for copy in copies:
        copy.start()
    target_ref, count_ref, old_ref, new_ref, mass_ref, vel_ref, delta_ref = staged
    rows, lanes = mass_ref.shape
    owners = out_ref.shape[0] // (CAP * FIELDS)
    levels = delta_ref.shape[0] // 3
    copies[0].wait()
    target = jnp.broadcast_to(target_ref[...], (owners, rows))
    marks = target == lax.broadcasted_iota(jnp.int32, (owners, rows), 0)
    before = lax.broadcasted_iota(jnp.int32, (rows, rows), 0) < lax.broadcasted_iota(jnp.int32, (rows, rows), 1)
    ones = jnp.where(marks, 1.0, 0.0)
    earlier = jnp.dot(
        ones.astype(jnp.bfloat16), jnp.where(before, 1.0, 0.0).astype(jnp.bfloat16), preferred_element_type=jnp.float32
    )
    for copy in copies[1:]:
        copy.wait()
    lane_index = lax.broadcasted_iota(jnp.int32, (lanes, lanes), 1).astype(jnp.float32)
    for part in range(rows // lanes):
        band = slice(part * lanes, (part + 1) * lanes)
        counts = jnp.broadcast_to(count_ref[:, band].astype(jnp.float32), (lanes, lanes)).T
        live_ref[band, :] = jnp.where(lane_index < counts, mass_ref[band, :], 0.0)
    step = 16

    def gather(index, carry):
        band = pl.ds(pl.multiple_of(index * step, step), step)
        cell = old_ref[band, :]
        along = cell & (lanes - 1)
        level = cell >> 7
        found = [jnp.zeros((step, lanes), jnp.float32)] * 3
        for h in range(levels):
            mask = level == h
            for c in range(3):
                table = jnp.broadcast_to(delta_ref[c * levels + h : c * levels + h + 1, :], (step, lanes))
                found[c] = jnp.where(mask, jnp.take_along_axis(table, along, axis=1), found[c])
        mass = live_ref[band, :]
        parts = [mass] + [mass * (vel_ref[c, band, :] + found[c]) for c in range(3)]
        parts.append(new_ref[band, :].astype(jnp.float32))
        for f, part in enumerate(parts):
            for k, piece in enumerate(pieces(part)):
                pay_ref[pl.ds(pl.multiple_of(k * rows + index * step, step), step), f * lanes : (f + 1) * lanes] = piece
        return carry

    lax.fori_loop(0, rows // step, gather, 0)
    for s in range(CAP):
        chosen = jnp.where(earlier == float(s), ones, 0.0).astype(jnp.bfloat16)
        picked = jnp.dot(jnp.concatenate([chosen] * 3, axis=1), pay_ref[...], preferred_element_type=jnp.float32)
        for f in range(FIELDS):
            out_ref[pl.ds(f * CAP + s, owners, stride=CAP * FIELDS), :] = picked[:, f * lanes : (f + 1) * lanes]


def pack(*args):
    rows, lanes = args[4].shape
    owners = lax.axis_size("gx") * lax.axis_size("gy")
    return pl.pallas_call(
        pack_kernel,
        out_shape=jax.ShapeDtypeStruct((owners * CAP * FIELDS, lanes), jnp.float32),
        in_specs=[pl.BlockSpec(memory_space=pltpu.MemorySpace.HBM)] * len(args),
        scratch_shapes=[pltpu.VMEM(a.shape, a.dtype) for a in args]
        + [
            pltpu.VMEM((rows, lanes), jnp.float32),
            pltpu.VMEM((3 * rows, FIELDS * lanes), jnp.bfloat16),
            pltpu.SemaphoreType.DMA((len(args),)),
        ],
        compiler_params=pltpu.CompilerParams(vmem_limit_bytes=16 << 20),
        name="pack",
    )(*[pltpu.with_memory_space_constraint(a, pltpu.MemorySpace.HBM) for a in args])


def whole(shape, value):
    return jnp.full(shape, value, jnp.bfloat16)


def row_index(shape):
    return lax.broadcasted_iota(jnp.int32, shape, 0).astype(jnp.float32).astype(jnp.bfloat16)


def deposit_kernel(in_ref, mass_ref, momentum_ref, field_ref, *rest):
    acc_ref = rest[-1]
    lanes = in_ref.shape[1]
    levels = mass_ref.shape[0]
    sources = in_ref.shape[0] // (CAP * FIELDS)
    group = 32
    acc_ref[...] = jnp.zeros_like(acc_ref)
    along_index = row_index((lanes, lanes))
    level_index = row_index((levels, lanes))

    def add(index, carry):
        lefts, rights = [], []
        for g in range(group):
            base = (index * group + g) * (CAP * FIELDS)
            for s in range(CAP):
                row = lambda f: in_ref[pl.ds(base + f * CAP + s, 1), :]
                cell = row(4).astype(jnp.int32)
                along = jnp.broadcast_to((cell & (lanes - 1)).astype(jnp.float32), (lanes, lanes)).astype(jnp.bfloat16)
                level = jnp.broadcast_to((cell >> 7).astype(jnp.float32), (levels, lanes)).astype(jnp.bfloat16)
                lefts.append(jnp.where(along == along_index, whole((lanes, lanes), 1.0), whole((lanes, lanes), 0.0)))
                here = level == level_index
                nothing = whole((levels, lanes), 0.0)
                tops, rests = [], []
                for c in range(4):
                    value = jnp.broadcast_to(row(c), (levels, lanes))
                    top = value.astype(jnp.bfloat16)
                    rest = (value - top.astype(jnp.float32)).astype(jnp.bfloat16)
                    tops.append(jnp.where(here, top, nothing))
                    rests.append(jnp.where(here, rest, nothing))
                rights.append(jnp.concatenate(tops + rests, axis=0))
        left = jnp.concatenate(lefts, axis=1)
        right = jnp.concatenate(rights, axis=1)
        acc_ref[...] += lax.dot_general(right, left, (((1,), (1,)), ((), ())), preferred_element_type=jnp.float32)
        return carry

    lax.fori_loop(0, sources // group, add, 0)
    half = 4 * levels
    sums = acc_ref[:half, :] + acc_ref[half:, :]
    finish(sums, mass_ref, momentum_ref, field_ref, *rest[:-1])


def finish(sums, mass_ref, momentum_ref, field_ref, inner_y_ref, outer_y_ref, inner_x_ref, outer_x_ref):
    levels, lanes = mass_ref.shape
    total = mass_ref[...] + sums[:levels]
    fields = [
        (momentum_ref[c * levels : (c + 1) * levels, :] + sums[(c + 1) * levels : (c + 2) * levels]) / total
        for c in range(3)
    ]
    fields.append(0.5 + 1.0 / total)
    rim = inner_x_ref.shape[0] // 4
    even_x = lax.axis_index("gx") % 2 == 0
    even_y = lax.axis_index("gy") % 2 == 0
    for f, field in enumerate(fields):
        field_ref[f * levels : (f + 1) * levels, :] = field
        low, high = field[:rim], field[levels - rim :]
        inner_x_ref[f * rim : (f + 1) * rim, :] = jnp.where(even_x, high, low)
        outer_x_ref[f * rim : (f + 1) * rim, :] = jnp.where(even_x, low, high)
    turned = jnp.concatenate(fields, axis=0).T
    low, high = turned[0:8], turned[lanes - 8 : lanes]
    inner_y_ref[...] = jnp.where(even_y, high, low)
    outer_y_ref[...] = jnp.where(even_y, low, high)


def deposit(incoming, fluid_mass, fluid_momentum):
    levels, lanes = fluid_mass.shape
    shapes = [(4 * levels, lanes), (8, lanes), (8, lanes), (4 * WIDTH * 4, lanes), (4 * WIDTH * 4, lanes)]
    vmem = pl.BlockSpec(memory_space=pltpu.MemorySpace.VMEM)
    return pl.pallas_call(
        deposit_kernel,
        out_shape=tuple(jax.ShapeDtypeStruct(shape, jnp.float32) for shape in shapes),
        in_specs=[vmem] * 3,
        scratch_shapes=[pltpu.VMEM((8 * levels, lanes), jnp.float32)],
        compiler_params=pltpu.CompilerParams(vmem_limit_bytes=24 << 20),
        name="deposit",
    )(incoming, fluid_mass, fluid_momentum)


def swaps(axis, outer, sizes):
    pairs = []
    for x in range(sizes[0]):
        for y in range(sizes[1]):
            here = [x, y]
            there = here[axis] + (1 if (here[axis] % 2 == 0) != outer else -1)
            if 0 <= there < sizes[axis]:
                here[axis] = there
            else:
                here[1 - axis] ^= 1
            pairs.append((x * sizes[1] + y, here[0] * sizes[1] + here[1]))
    return pairs


def solve_kernel(sizes, field_ref, inner_y_ref, outer_y_ref, inner_x_ref, outer_x_ref, vel_ref, out_ref, sem):
    copy = pltpu.make_async_copy(field_ref.at[: vel_ref.shape[0]], vel_ref, sem)
    copy.start()
    depth = 4
    lanes = out_ref.shape[1]
    levels = out_ref.shape[0]
    rim = WIDTH * depth
    faces = 4 * rim
    zero = jnp.zeros((lanes - 16, lanes), jnp.float32)

    x, y = lax.axis_index("gx"), lax.axis_index("gy")
    even_x, even_y = x % 2 == 0, y % 2 == 0
    has_below, has_above = x > 0, x < sizes[0] - 1
    has_left, has_right = y > 0, y < sizes[1] - 1

    def sidewise(inner, outer):
        right = jnp.where(has_right, jnp.where(even_y, inner, outer), 0.0)
        left = jnp.where(has_left, jnp.where(even_y, outer, inner), 0.0)
        return jnp.concatenate([right, zero, left], axis=0).T

    inner_x, outer_x = inner_x_ref[...], outer_x_ref[...]
    below = jnp.where(has_below, jnp.where(even_x, outer_x, inner_x), 0.0)
    above = jnp.where(has_above, jnp.where(even_x, inner_x, outer_x), 0.0)
    own_side = sidewise(inner_y_ref[...], outer_y_ref[...])
    below_side = sidewise(below[faces : faces + 8], below[faces + 8 :])
    above_side = sidewise(above[faces : faces + 8], above[faces + 8 :])
    wide = []
    near = (lax.broadcasted_iota(jnp.int32, (levels + 2 * rim, lanes), 1) < WIDTH) | (
        lax.broadcasted_iota(jnp.int32, (levels + 2 * rim, lanes), 1) >= lanes - WIDTH
    )
    for f in range(4):
        first = jnp.concatenate(
            [below[f * rim : (f + 1) * rim], field_ref[f * levels : (f + 1) * levels, :], above[f * rim : (f + 1) * rim]], axis=0
        )
        second = jnp.concatenate(
            [
                below_side[(f + 1) * levels - rim : (f + 1) * levels],
                own_side[f * levels : (f + 1) * levels],
                above_side[f * levels : f * levels + rim],
            ],
            axis=0,
        )
        wide.append(jnp.concatenate([first, jnp.where(near, second, 0.0)], axis=1))
    u, v, w, stiffness = wide
    total_rows = levels + 2 * rim

    def roll_rows(value, amount):
        return pltpu.roll(value, amount % total_rows, 0)

    def roll_lanes(value, amount):
        return pltpu.roll(value, amount % (2 * lanes), 1)

    row = lax.broadcasted_iota(jnp.int32, (total_rows, 2 * lanes), 0)
    z = row % depth

    def above_z(value):
        return jnp.where(z == depth - 1, 0.0, roll_rows(value, -1))

    def below_z(value):
        return jnp.where(z == 0, 0.0, roll_rows(value, 1))

    inside = stiffness > 0.0
    source = -0.5 * (
        (roll_rows(u, -depth) - roll_rows(u, depth))
        + (roll_lanes(v, -1) - roll_lanes(v, 1))
        + (above_z(w) - below_z(w))
    )
    source = jnp.where(inside, source, 0.0)
    theta = (eigen_high + eigen_low) / 2.0
    delta = (eigen_high - eigen_low) / 2.0
    sigma = theta / delta
    rho = 1.0 / sigma
    pressure = jnp.zeros_like(source)
    residual = source
    search = source / theta
    for sweep in range(SWEEPS):
        pressure = pressure + search
        if sweep + 1 < SWEEPS:
            beside = (
                roll_rows(search, -depth) + roll_rows(search, depth)
                + roll_lanes(search, -1) + roll_lanes(search, 1)
                + above_z(search) + below_z(search)
            )
            residual = residual - ((6.0 + stiffness) * search - beside)
            rho_new = 1.0 / (2.0 * sigma - rho)
            search = rho_new * rho * search + 2.0 * rho_new / delta * residual
            search = jnp.where(inside, search, 0.0)
            rho = rho_new
    out_ref[...] = pressure[rim : rim + levels, :lanes]
    copy.wait()


def local(destination, row_count, old_cell, new_cell, point_mass, point_vel, grid_delta, fluid_mass, fluid_momentum):
    rows, lanes = point_mass.shape
    across, depth, along = fluid_mass.shape
    levels = across * depth
    sizes = (lax.axis_size("gx"), lax.axis_size("gy"))
    owners = sizes[0] * sizes[1]
    outgoing = pack(
        destination.reshape(1, rows),
        row_count.reshape(1, rows),
        old_cell,
        new_cell,
        point_mass,
        jnp.swapaxes(point_vel, 0, 1),
        grid_delta.reshape(3 * levels, along),
    )
    incoming = lax.all_to_all(
        outgoing.reshape(owners, 1, CAP * FIELDS * lanes), ("gx", "gy"), split_axis=0, concat_axis=0, tiled=True
    ).reshape(owners * CAP * FIELDS, lanes)
    fields, inner_y, outer_y, inner_x, outer_x = deposit(
        incoming, fluid_mass.reshape(levels, along), fluid_momentum.reshape(3 * levels, along)
    )

    def swap(value, axis, outer):
        return lax.ppermute(value, ("gx", "gy"), swaps(axis, outer, sizes))

    inner_y = swap(inner_y, 1, False)
    outer_y = swap(outer_y, 1, True)
    inner_x = swap(jnp.concatenate([inner_x, inner_y, outer_y], axis=0), 0, False)
    outer_x = swap(jnp.concatenate([outer_x, inner_y, outer_y], axis=0), 0, True)
    vmem = pl.BlockSpec(memory_space=pltpu.MemorySpace.VMEM)
    velocity, pressure = pl.pallas_call(
        functools.partial(solve_kernel, sizes),
        out_shape=(
            jax.ShapeDtypeStruct((3 * levels, along), jnp.float32),
            jax.ShapeDtypeStruct((levels, along), jnp.float32),
        ),
        in_specs=[vmem] * 5,
        out_specs=(pl.BlockSpec(memory_space=pltpu.MemorySpace.HBM), vmem),
        scratch_shapes=[pltpu.SemaphoreType.DMA],
        compiler_params=pltpu.CompilerParams(vmem_limit_bytes=8 << 20),
        name="solve",
    )(fields, inner_y, outer_y, inner_x, outer_x)
    return velocity.reshape(3, across, depth, along), pressure.reshape(across, depth, along)


def solution(mesh):
    return jax.shard_map(
        local,
        mesh=mesh,
        in_specs=(
            P(("gx", "gy"), None),
            P(("gx", "gy")),
            P(("gx", "gy"), None),
            P(("gx", "gy"), None),
            P(("gx", "gy"), None),
            P(("gx", "gy"), None, None),
            P(None, "gx", None, "gy"),
            P("gx", None, "gy"),
            P(None, "gx", None, "gy"),
        ),
        out_specs=(P(None, "gx", None, "gy"), P("gx", None, "gy")),
        check_vma=False,
    )
```

```python
import functools

import jax
import jax.numpy as jnp
from jax import lax
from jax.experimental import pallas as pl
from jax.experimental.pallas import tpu as pltpu
from jax.sharding import PartitionSpec as P

CAP = 3
FIELDS = 5
SWEEPS = 4
WIDTH = 4
PLANES = (4, 3, 3, 2)

eigen_low = 0.5
eigen_high = 14.5


def iota_bf(shape):
    return lax.broadcasted_iota(jnp.int32, shape, 0).astype(jnp.float32).astype(jnp.bfloat16)

def deposit_kernel(group, form, in_ref, mass_ref, momentum_ref, vel_ref, field_ref, low_ref, high_ref, down_ref, up_ref, acc_ref):
    lanes = in_ref.shape[1]
    levels = mass_ref.shape[0]
    sources = in_ref.shape[0] // (CAP * FIELDS)
    acc_ref[...] = jnp.zeros_like(acc_ref)
    along_index = iota_bf((lanes, lanes))
    level_index = iota_bf((levels, lanes))

    def add(index, carry):
        lefts, rights = [], []
        for g in range(group):
            base = (index * group + g) * (CAP * FIELDS)
            for s in range(CAP):
                row = lambda f: in_ref[pl.ds(base + f * CAP + s, 1), :]
                cell = row(4).astype(jnp.int32)
                along = jnp.broadcast_to((cell & (lanes - 1)).astype(jnp.float32), (lanes, lanes)).astype(jnp.bfloat16)
                level = jnp.broadcast_to((cell >> 7).astype(jnp.float32), (levels, lanes)).astype(jnp.bfloat16)
                lefts.append(jnp.where(along == along_index, jnp.ones((lanes, lanes), jnp.bfloat16), jnp.zeros((lanes, lanes), jnp.bfloat16)))
                here = level == level_index
                nothing = jnp.zeros((levels, lanes), jnp.bfloat16)
                tops, rests = [], []
                for c in range(4):
                    value = jnp.broadcast_to(row(c), (levels, lanes))
                    top = value.astype(jnp.bfloat16)
                    rest = (value - top.astype(jnp.float32)).astype(jnp.bfloat16)
                    tops.append(jnp.where(here, top, nothing))
                    rests.append(jnp.where(here, rest, nothing))
                rights.append(jnp.concatenate(tops + rests, axis=0))
        left = jnp.concatenate(lefts, axis=1)
        right = jnp.concatenate(rights, axis=1)
        if form == "NT":
            acc_ref[...] += lax.dot_general(left, right, (((1,), (1,)), ((), ())), preferred_element_type=jnp.float32)
        else:
            acc_ref[...] += lax.dot_general(right, left, (((1,), (1,)), ((), ())), preferred_element_type=jnp.float32)
        return carry

    lax.fori_loop(0, sources // group, add, 0)
    half = 4 * levels
    if form == "NT":
        sums = (acc_ref[:, :half] + acc_ref[:, half:]).T
    else:
        sums = acc_ref[:half, :] + acc_ref[half:, :]
    total = mass_ref[...] + sums[:levels]
    inverse = 1.0 / total
    fields = []
    for c in range(3):
        value = (momentum_ref[c * levels : (c + 1) * levels, :] + sums[(c + 1) * levels : (c + 2) * levels]) / total
        vel_ref[c * levels : (c + 1) * levels, :] = value
        field_ref[c * levels : (c + 1) * levels, :] = value
        fields.append(value)
    stiffness = 0.5 + inverse
    field_ref[3 * levels : 4 * levels, :] = stiffness
    fields.append(stiffness)
    turned = jnp.concatenate(fields, axis=0).T
    low_ref[...] = turned[0:8]
    high_ref[...] = turned[lanes - 8 : lanes]
    rim = down_ref.shape[1]
    for f in range(4):
        down_ref[f] = fields[f][:rim]
        up_ref[f] = fields[f][levels - rim :]

def deposit(incoming, fluid_mass, fluid_momentum, group=8, form="NTs", name="deposit", vmem=24<<20):
    levels, lanes = fluid_mass.shape
    return pl.pallas_call(
        functools.partial(deposit_kernel, group, form),
        out_shape=(
            jax.ShapeDtypeStruct((3 * levels, lanes), jnp.float32),
            jax.ShapeDtypeStruct((4 * levels, lanes), jnp.float32),
            jax.ShapeDtypeStruct((8, lanes), jnp.float32),
            jax.ShapeDtypeStruct((8, lanes), jnp.float32),
            jax.ShapeDtypeStruct((4, WIDTH * 4, lanes), jnp.float32),
            jax.ShapeDtypeStruct((4, WIDTH * 4, lanes), jnp.float32),
        ),
        scratch_shapes=[pltpu.VMEM((lanes, 8 * levels) if form == "NT" else (8 * levels, lanes), jnp.float32)],
        compiler_params=pltpu.CompilerParams(vmem_limit_bytes=vmem),
        name=name,
    )(incoming, fluid_mass, fluid_momentum)

def pieces(value):
    top = value.astype(jnp.bfloat16)
    return top, (value - top.astype(jnp.float32)).astype(jnp.bfloat16)


def pack_kernel(*refs):
    inputs, out_ref, staged, (live_ref, pay_ref, sem) = refs[:7], refs[7], refs[8:15], refs[15:]
    copies = [pltpu.make_async_copy(src, dst, sem.at[i]) for i, (src, dst) in enumerate(zip(inputs, staged))]
    for copy in copies:
        copy.start()
    target_ref, count_ref, old_ref, new_ref, mass_ref, vel_ref, delta_ref = staged
    rows, lanes = mass_ref.shape
    owners = out_ref.shape[0] // (CAP * FIELDS)
    levels = delta_ref.shape[0] // 3
    copies[0].wait()
    target = jnp.broadcast_to(target_ref[...], (owners, rows))
    marks = target == lax.broadcasted_iota(jnp.int32, (owners, rows), 0)
    before = lax.broadcasted_iota(jnp.int32, (rows, rows), 0) < lax.broadcasted_iota(jnp.int32, (rows, rows), 1)
    ones = jnp.where(marks, 1.0, 0.0)
    earlier = jnp.dot(
        ones.astype(jnp.bfloat16), jnp.where(before, 1.0, 0.0).astype(jnp.bfloat16), preferred_element_type=jnp.float32
    )
    for copy in copies[1:]:
        copy.wait()
    lane_index = lax.broadcasted_iota(jnp.int32, (lanes, lanes), 1).astype(jnp.float32)
    for part in range(rows // lanes):
        band = slice(part * lanes, (part + 1) * lanes)
        counts = jnp.broadcast_to(count_ref[:, band].astype(jnp.float32), (lanes, lanes)).T
        live_ref[band, :] = jnp.where(lane_index < counts, mass_ref[band, :], 0.0)
    step = 16

    def gather(index, carry):
        band = pl.ds(pl.multiple_of(index * step, step), step)
        cell = old_ref[band, :]
        along = cell & (lanes - 1)
        level = cell >> 7
        found = [jnp.zeros((step, lanes), jnp.float32)] * 3
        for c in range(3):
            for h in range(levels):
                table = jnp.broadcast_to(delta_ref[c * levels + h : c * levels + h + 1, :], (step, lanes))
                found[c] = jnp.where(level == h, jnp.take_along_axis(table, along, axis=1), found[c])
        mass = live_ref[band, :]
        parts = [mass] + [mass * (vel_ref[c, band, :] + found[c]) for c in range(3)]
        parts.append(new_ref[band, :].astype(jnp.float32))
        for f, part in enumerate(parts):
            for k, piece in enumerate(pieces(part)):
                pay_ref[pl.ds(pl.multiple_of(k * rows + index * step, step), step), f * lanes : (f + 1) * lanes] = piece
        return carry

    lax.fori_loop(0, rows // step, gather, 0)
    for s in range(CAP):
        chosen = jnp.where(earlier == float(s), ones, 0.0).astype(jnp.bfloat16)
        picked = jnp.dot(jnp.concatenate([chosen] * 2, axis=1), pay_ref[...], preferred_element_type=jnp.float32)
        for f in range(FIELDS):
            out_ref[pl.ds(f * CAP + s, owners, stride=CAP * FIELDS), :] = picked[:, f * lanes : (f + 1) * lanes]


def pack(*args):
    rows, lanes = args[4].shape
    owners = lax.axis_size("gx") * lax.axis_size("gy")
    return pl.pallas_call(
        pack_kernel,
        out_shape=jax.ShapeDtypeStruct((owners * CAP * FIELDS, lanes), jnp.float32),
        in_specs=[pl.BlockSpec(memory_space=pltpu.MemorySpace.HBM)] * len(args),
        scratch_shapes=[pltpu.VMEM(a.shape, a.dtype) for a in args]
        + [
            pltpu.VMEM((rows, lanes), jnp.float32),
            pltpu.VMEM((2 * rows, FIELDS * lanes), jnp.bfloat16),
            pltpu.SemaphoreType.DMA((len(args),)),
        ],
        compiler_params=pltpu.CompilerParams(vmem_limit_bytes=16 << 20),
        name="pack",
    )(*[pltpu.with_memory_space_constraint(a, pltpu.MemorySpace.HBM) for a in args])


def whole(shape, value):
    return jnp.full(shape, value, jnp.bfloat16)


def row_index(shape):
    return lax.broadcasted_iota(jnp.int32, shape, 0).astype(jnp.float32).astype(jnp.bfloat16)


def deposit_kernel(in_ref, mass_ref, momentum_ref, field_ref, *rest):
    acc_ref = rest[-1]
    lanes = in_ref.shape[1]
    levels = mass_ref.shape[0]
    sources = in_ref.shape[0] // (CAP * FIELDS)
    group = 64
    acc_ref[...] = jnp.zeros_like(acc_ref)
    along_index = row_index((lanes, lanes))
    level_index = row_index((levels, lanes))

    def add(index, carry):
        lefts, rights = [], []
        for g in range(group):
            base = (index * group + g) * (CAP * FIELDS)
            for s in range(CAP):
                row = lambda f: in_ref[pl.ds(base + f * CAP + s, 1), :]
                cell = row(4).astype(jnp.int32)
                along = jnp.broadcast_to((cell & (lanes - 1)).astype(jnp.float32), (lanes, lanes)).astype(jnp.bfloat16)
                level = jnp.broadcast_to((cell >> 7).astype(jnp.float32), (levels, lanes)).astype(jnp.bfloat16)
                lefts.append(jnp.where(along == along_index, whole((lanes, lanes), 1.0), whole((lanes, lanes), 0.0)))
                here = level == level_index
                nothing = whole((levels, lanes), 0.0)
                tops, rests = [], []
                for c in range(4):
                    value = jnp.broadcast_to(row(c), (levels, lanes))
                    top = value.astype(jnp.bfloat16)
                    rest = (value - top.astype(jnp.float32)).astype(jnp.bfloat16)
                    tops.append(jnp.where(here, top, nothing))
                    rests.append(jnp.where(here, rest, nothing))
                rights.append(jnp.concatenate(tops + rests, axis=0))
        left = jnp.concatenate(lefts, axis=1)
        right = jnp.concatenate(rights, axis=1)
        acc_ref[...] += lax.dot_general(right, left, (((1,), (1,)), ((), ())), preferred_element_type=jnp.float32)
        return carry

    lax.fori_loop(0, sources // group, add, 0)
    half = 4 * levels
    sums = acc_ref[:half, :] + acc_ref[half:, :]
    finish(sums, mass_ref, momentum_ref, field_ref, *rest[:-1])


def finish(sums, mass_ref, momentum_ref, field_ref, inner_y_ref, outer_y_ref, inner_x_ref, outer_x_ref):
    levels, lanes = mass_ref.shape
    total = mass_ref[...] + sums[:levels]
    fields = [
        (momentum_ref[c * levels : (c + 1) * levels, :] + sums[(c + 1) * levels : (c + 2) * levels]) / total
        for c in range(3)
    ]
    fields.append(0.5 + 1.0 / total)
    plane = inner_x_ref.shape[0] // sum(PLANES)
    start = 0
    even_x = lax.axis_index("gx") % 2 == 0
    even_y = lax.axis_index("gy") % 2 == 0
    for f, field in enumerate(fields):
        field_ref[f * levels : (f + 1) * levels, :] = field
        rim = PLANES[f] * plane
        low, high = field[:rim], field[levels - rim :]
        inner_x_ref[start : start + rim, :] = jnp.where(even_x, high, low)
        outer_x_ref[start : start + rim, :] = jnp.where(even_x, low, high)
        start += rim
    turned = jnp.concatenate(fields, axis=0).T
    low, high = turned[:WIDTH], turned[lanes - WIDTH :]
    inner_y_ref[...] = jnp.where(even_y, high, low)
    outer_y_ref[...] = jnp.where(even_y, low, high)


def deposit(incoming, fluid_mass, fluid_momentum):
    levels, lanes = fluid_mass.shape
    shapes = [(4 * levels, lanes)] + [(WIDTH, lanes)] * 2 + [(sum(PLANES) * 4, lanes)] * 2
    vmem = pl.BlockSpec(memory_space=pltpu.MemorySpace.VMEM)
    return pl.pallas_call(
        deposit_kernel,
        out_shape=tuple(jax.ShapeDtypeStruct(shape, jnp.float32) for shape in shapes),
        in_specs=[vmem] * 3,
        scratch_shapes=[pltpu.VMEM((8 * levels, lanes), jnp.float32)],
        compiler_params=pltpu.CompilerParams(vmem_limit_bytes=36 << 20),
        name="deposit",
    )(incoming, fluid_mass, fluid_momentum)


def swaps(axis, outer, sizes):
    pairs = []
    for x in range(sizes[0]):
        for y in range(sizes[1]):
            here = [x, y]
            there = here[axis] + (1 if (here[axis] % 2 == 0) != outer else -1)
            if 0 <= there < sizes[axis]:
                here[axis] = there
            else:
                here[1 - axis] ^= 1
            pairs.append((x * sizes[1] + y, here[0] * sizes[1] + here[1]))
    return pairs


def solve_kernel(sizes, field_ref, inner_y_ref, outer_y_ref, inner_x_ref, outer_x_ref, inner_c_ref, outer_c_ref, vel_ref, out_ref, sem):
    copy = pltpu.make_async_copy(field_ref.at[: vel_ref.shape[0]], vel_ref, sem)
    copy.start()
    depth = 4
    lanes = out_ref.shape[1]
    levels = out_ref.shape[0]
    rim = WIDTH * depth
    zero = jnp.zeros((lanes - 2 * WIDTH, lanes), jnp.float32)

    x, y = lax.axis_index("gx"), lax.axis_index("gy")
    even_x, even_y = x % 2 == 0, y % 2 == 0
    has_below, has_above = x > 0, x < sizes[0] - 1
    has_left, has_right = y > 0, y < sizes[1] - 1

    def sidewise(inner, outer):
        right = jnp.where(has_right, jnp.where(even_y, inner, outer), 0.0)
        left = jnp.where(has_left, jnp.where(even_y, outer, inner), 0.0)
        return jnp.concatenate([right, zero, left], axis=0).T

    inner_x, outer_x = inner_x_ref[...], outer_x_ref[...]
    below = jnp.where(has_below, jnp.where(even_x, outer_x, inner_x), 0.0)
    above = jnp.where(has_above, jnp.where(even_x, inner_x, outer_x), 0.0)
    inner_c, outer_c = inner_c_ref[...], outer_c_ref[...]
    below_c = jnp.where(has_below, jnp.where(even_x, outer_c, inner_c), 0.0)
    above_c = jnp.where(has_above, jnp.where(even_x, inner_c, outer_c), 0.0)
    own_side = sidewise(inner_y_ref[...], outer_y_ref[...])
    below_side = sidewise(below_c[:WIDTH], below_c[WIDTH:])
    above_side = sidewise(above_c[:WIDTH], above_c[WIDTH:])
    wide = []
    start = 0
    for f in range(4):
        kept = PLANES[f] * depth
        rows = [field_ref[f * levels : (f + 1) * levels, :]]
        if kept < rim:
            gap = jnp.zeros((rim - kept, lanes), jnp.float32)
            rows = [gap, below[start : start + kept]] + rows + [above[start : start + kept], gap]
        else:
            rows = [below[start : start + kept]] + rows + [above[start : start + kept]]
        start += kept
        second = jnp.concatenate(
            [
                below_side[(f + 1) * levels - rim : (f + 1) * levels],
                own_side[f * levels : (f + 1) * levels],
                above_side[f * levels : f * levels + rim],
            ],
            axis=0,
        )
        wide.append(jnp.concatenate([jnp.concatenate(rows, axis=0), second], axis=1))
    u, v, w, stiffness = wide
    total_rows = levels + 2 * rim

    def roll_rows(value, amount):
        return pltpu.roll(value, amount % total_rows, 0)

    def roll_lanes(value, amount):
        return pltpu.roll(value, amount % (2 * lanes), 1)

    row = lax.broadcasted_iota(jnp.int32, (total_rows, 2 * lanes), 0)
    z = row % depth

    def above_z(value):
        return jnp.where(z == depth - 1, 0.0, roll_rows(value, -1))

    def below_z(value):
        return jnp.where(z == 0, 0.0, roll_rows(value, 1))

    lane = lax.broadcasted_iota(jnp.int32, (total_rows, 2 * lanes), 1)
    first_row, last_row = jnp.where(has_below, 0, rim), jnp.where(has_above, total_rows, rim + levels)
    last_lane = jnp.where(has_right, lanes + WIDTH, lanes)
    first_left = jnp.where(has_left, 2 * lanes - WIDTH, 2 * lanes)
    inside = (row >= first_row) & (row < last_row) & ((lane < last_lane) | (lane >= first_left))
    source = -0.5 * (
        (roll_rows(u, -depth) - roll_rows(u, depth))
        + (roll_lanes(v, -1) - roll_lanes(v, 1))
        + (above_z(w) - below_z(w))
    )
    source = jnp.where(inside, source, 0.0)
    theta = (eigen_high + eigen_low) / 2.0
    delta = (eigen_high - eigen_low) / 2.0
    sigma = theta / delta
    rho = 1.0 / sigma
    pressure = jnp.zeros_like(source)
    residual = source
    search = source / theta
    for sweep in range(SWEEPS):
        pressure = pressure + search
        if sweep + 1 < SWEEPS:
            beside = (
                roll_rows(search, -depth) + roll_rows(search, depth)
                + roll_lanes(search, -1) + roll_lanes(search, 1)
                + above_z(search) + below_z(search)
            )
            residual = residual - ((6.0 + stiffness) * search - beside)
            rho_new = 1.0 / (2.0 * sigma - rho)
            search = rho_new * rho * search + 2.0 * rho_new / delta * residual
            search = jnp.where(inside, search, 0.0)
            rho = rho_new
    out_ref[...] = pressure[rim : rim + levels, :lanes]
    copy.wait()


def local(destination, row_count, old_cell, new_cell, point_mass, point_vel, grid_delta, fluid_mass, fluid_momentum):
    rows, lanes = point_mass.shape
    across, depth, along = fluid_mass.shape
    levels = across * depth
    sizes = (lax.axis_size("gx"), lax.axis_size("gy"))
    owners = sizes[0] * sizes[1]
    outgoing = pack(
        destination.reshape(1, rows),
        row_count.reshape(1, rows),
        old_cell,
        new_cell,
        point_mass,
        jnp.swapaxes(point_vel, 0, 1),
        grid_delta.reshape(3 * levels, along),
    )
    incoming = lax.all_to_all(
        outgoing.reshape(owners, 1, CAP * FIELDS * lanes), ("gx", "gy"), split_axis=0, concat_axis=0, tiled=True
    ).reshape(owners * CAP * FIELDS, lanes)
    fields, inner_y, outer_y, inner_x, outer_x = deposit(
        incoming, fluid_mass.reshape(levels, along), fluid_momentum.reshape(3 * levels, along)
    )

    def swap(value, axis, outer):
        return lax.ppermute(value, ("gx", "gy"), swaps(axis, outer, sizes))

    inner_y = swap(inner_y, 1, False)
    outer_y = swap(outer_y, 1, True)
    inner_x = swap(inner_x, 0, False)
    outer_x = swap(outer_x, 0, True)
    columns = jnp.concatenate([inner_y, outer_y], axis=0)
    inner_c = swap(columns, 0, False)
    outer_c = swap(columns, 0, True)
    vmem = pl.BlockSpec(memory_space=pltpu.MemorySpace.VMEM)
    velocity, pressure = pl.pallas_call(
        functools.partial(solve_kernel, sizes),
        out_shape=(
            jax.ShapeDtypeStruct((3 * levels, along), jnp.float32),
            jax.ShapeDtypeStruct((levels, along), jnp.float32),
        ),
        in_specs=[vmem] * 7,
        out_specs=(pl.BlockSpec(memory_space=pltpu.MemorySpace.HBM), vmem),
        scratch_shapes=[pltpu.SemaphoreType.DMA],
        compiler_params=pltpu.CompilerParams(vmem_limit_bytes=8 << 20),
        name="solve",
    )(fields, inner_y, outer_y, inner_x, outer_x, inner_c, outer_c)
    return velocity.reshape(3, across, depth, along), pressure.reshape(across, depth, along)


def solution(mesh):
    return jax.shard_map(
        local,
        mesh=mesh,
        in_specs=(
            P(("gx", "gy"), None),
            P(("gx", "gy")),
            P(("gx", "gy"), None),
            P(("gx", "gy"), None),
            P(("gx", "gy"), None),
            P(("gx", "gy"), None, None),
            P(None, "gx", None, "gy"),
            P("gx", None, "gy"),
            P(None, "gx", None, "gy"),
        ),
        out_specs=(P(None, "gx", None, "gy"), P("gx", None, "gy")),
        check_vma=False,
    )
```

```python
import functools

import jax
import jax.numpy as jnp
from jax import lax
from jax.experimental import pallas as pl
from jax.experimental.pallas import tpu as pltpu
from jax.sharding import PartitionSpec as P

CAP = 3
FIELDS = 5
SWEEPS = 4
WIDTH = 4
PLANES = (4, 3, 3, 2)
HIGH = 24
LOW = 192
GROUP = 64

eigen_low = 0.5
eigen_high = 14.5


def pieces(value):
    top = value.astype(jnp.bfloat16)
    return top, (value - top.astype(jnp.float32)).astype(jnp.bfloat16)


def pack_kernel(*refs):
    inputs, out_ref, staged, (live_ref, pay_ref, sem) = refs[:7], refs[7], refs[8:15], refs[15:]
    copies = [pltpu.make_async_copy(src, dst, sem.at[i]) for i, (src, dst) in enumerate(zip(inputs, staged))]
    for copy in copies:
        copy.start()
    target_ref, count_ref, old_ref, new_ref, mass_ref, vel_ref, delta_ref = staged
    rows, lanes = mass_ref.shape
    owners = out_ref.shape[0] // (CAP * FIELDS)
    levels = delta_ref.shape[0] // 3
    copies[0].wait()
    target = jnp.broadcast_to(target_ref[...], (owners, rows))
    marks = target == lax.broadcasted_iota(jnp.int32, (owners, rows), 0)
    before = lax.broadcasted_iota(jnp.int32, (rows, rows), 0) < lax.broadcasted_iota(jnp.int32, (rows, rows), 1)
    ones = jnp.where(marks, 1.0, 0.0)
    earlier = jnp.dot(
        ones.astype(jnp.bfloat16), jnp.where(before, 1.0, 0.0).astype(jnp.bfloat16), preferred_element_type=jnp.float32
    )
    for copy in copies[1:]:
        copy.wait()
    lane_index = lax.broadcasted_iota(jnp.int32, (lanes, lanes), 1).astype(jnp.float32)
    for part in range(rows // lanes):
        band = slice(part * lanes, (part + 1) * lanes)
        counts = jnp.broadcast_to(count_ref[:, band].astype(jnp.float32), (lanes, lanes)).T
        live_ref[band, :] = jnp.where(lane_index < counts, mass_ref[band, :], 0.0)
    step = 16

    def gather(index, carry):
        band = pl.ds(pl.multiple_of(index * step, step), step)
        cell = old_ref[band, :]
        along = cell & (lanes - 1)
        level = cell >> 7
        found = [jnp.zeros((step, lanes), jnp.float32)] * 3
        for c in range(3):
            for h in range(levels):
                table = jnp.broadcast_to(delta_ref[c * levels + h : c * levels + h + 1, :], (step, lanes))
                found[c] = jnp.where(level == h, jnp.take_along_axis(table, along, axis=1), found[c])
        mass = live_ref[band, :]
        parts = [mass] + [mass * (vel_ref[c, band, :] + found[c]) for c in range(3)]
        parts.append(new_ref[band, :].astype(jnp.float32))
        for f, part in enumerate(parts):
            for k, piece in enumerate(pieces(part)):
                pay_ref[pl.ds(pl.multiple_of(k * rows + index * step, step), step), f * lanes : (f + 1) * lanes] = piece
        return carry

    lax.fori_loop(0, rows // step, gather, 0)
    for s in range(CAP):
        chosen = jnp.where(earlier == float(s), ones, 0.0).astype(jnp.bfloat16)
        picked = jnp.dot(jnp.concatenate([chosen] * 2, axis=1), pay_ref[...], preferred_element_type=jnp.float32)
        for f in range(FIELDS):
            out_ref[pl.ds(f * CAP + s, owners, stride=CAP * FIELDS), :] = picked[:, f * lanes : (f + 1) * lanes]


def pack(*args):
    rows, lanes = args[4].shape
    owners = lax.axis_size("gx") * lax.axis_size("gy")
    return pl.pallas_call(
        pack_kernel,
        out_shape=jax.ShapeDtypeStruct((owners * CAP * FIELDS, lanes), jnp.float32),
        in_specs=[pl.BlockSpec(memory_space=pltpu.MemorySpace.HBM)] * len(args),
        scratch_shapes=[pltpu.VMEM(a.shape, a.dtype) for a in args]
        + [
            pltpu.VMEM((rows, lanes), jnp.float32),
            pltpu.VMEM((2 * rows, FIELDS * lanes), jnp.bfloat16),
            pltpu.SemaphoreType.DMA((len(args),)),
        ],
        compiler_params=pltpu.CompilerParams(vmem_limit_bytes=16 << 20),
        name="pack",
    )(*[pltpu.with_memory_space_constraint(a, pltpu.MemorySpace.HBM) for a in args])


def whole(shape, value):
    return jnp.full(shape, value, jnp.bfloat16)


def row_index(shape):
    return lax.broadcasted_iota(jnp.int32, shape, 0).astype(jnp.float32).astype(jnp.bfloat16)


def deposit_kernel(in_ref, mass_ref, momentum_ref, field_ref, *rest):
    acc_ref, turn_ref = rest[-2:]
    lanes = in_ref.shape[1]
    sources = in_ref.shape[0] // (CAP * FIELDS)
    group = GROUP
    acc_ref[...] = jnp.zeros_like(acc_ref)
    low_index = row_index((LOW, lanes))
    high_index = jnp.concatenate([lax.broadcasted_iota(jnp.int32, (HIGH, lanes), 0)] * 2, axis=0)
    high_index = high_index.astype(jnp.float32).astype(jnp.bfloat16)
    one, zero = whole((LOW, lanes), 1.0), whole((LOW, lanes), 0.0)
    nothing = whole((2 * HIGH, lanes), 0.0)

    def add(index, carry):
        lefts, rights = [], []
        for g in range(group):
            base = (index * group + g) * (CAP * FIELDS)
            for s in range(CAP):
                row = lambda f: in_ref[pl.ds(base + f * CAP + s, 1), :]
                cell = row(4).astype(jnp.int32)
                high = ((cell >> 6) * 171) >> 9
                low = (cell - high * LOW).astype(jnp.float32)
                low = jnp.broadcast_to(low, (LOW, lanes)).astype(jnp.bfloat16)
                high = jnp.broadcast_to(high.astype(jnp.float32), (2 * HIGH, lanes)).astype(jnp.bfloat16)
                lefts.append(jnp.where(low == low_index, one, zero))
                here = high == high_index
                for c in range(4):
                    value = row(c)
                    top = value.astype(jnp.bfloat16).astype(jnp.float32)
                    both = [jnp.broadcast_to(piece, (HIGH, lanes)) for piece in (top, value - top)]
                    rights.append(jnp.where(here, jnp.concatenate(both, axis=0).astype(jnp.bfloat16), nothing))
        left = jnp.concatenate(lefts, axis=1)
        right = jnp.concatenate(
            [jnp.concatenate(rights[4 * i : 4 * i + 4], axis=0) for i in range(len(lefts))], axis=1
        )
        acc_ref[...] += lax.dot_general(right, left, (((1,), (1,)), ((), ())), preferred_element_type=jnp.float32)
        return carry

    lax.fori_loop(0, sources // group, add, 0)
    for c in range(4):
        part = acc_ref[2 * c * HIGH : (2 * c + 1) * HIGH, :] + acc_ref[(2 * c + 1) * HIGH : (2 * c + 2) * HIGH, :]
        turn_ref[0, c * HIGH : (c + 1) * HIGH, :] = part[:, :lanes]
        turn_ref[1, c * HIGH : (c + 1) * HIGH, : LOW - lanes] = part[:, lanes:]
    pairs = 2 * HIGH
    half = lanes // 2
    even, odd = pl.ds(0, pairs, stride=2), pl.ds(1, pairs, stride=2)
    cells_ref = rest[-3]
    cells_ref[pl.ds(0, pairs, stride=3), :] = turn_ref[0, even, :]
    odd_row = turn_ref[0, odd, :]
    cells_ref[pl.ds(1, pairs, stride=3), :] = jnp.concatenate([turn_ref[1, even, :][:, :half], odd_row[:, :half]], axis=1)
    cells_ref[pl.ds(2, pairs, stride=3), :] = jnp.concatenate([odd_row[:, half:], turn_ref[1, odd, :][:, :half]], axis=1)
    levels = mass_ref.shape[0]
    span = HIGH * LOW // lanes
    sums = [cells_ref[c * span : c * span + levels, :] for c in range(4)]
    finish(sums, mass_ref, momentum_ref, field_ref, *rest[:-3])


def finish(sums, mass_ref, momentum_ref, field_ref, inner_y_ref, outer_y_ref, inner_x_ref, outer_x_ref):
    levels, lanes = mass_ref.shape
    total = mass_ref[...] + sums[0]
    fields = [
        (momentum_ref[c * levels : (c + 1) * levels, :] + sums[c + 1]) / total
        for c in range(3)
    ]
    fields.append(0.5 + 1.0 / total)
    plane = inner_x_ref.shape[0] // sum(PLANES)
    start = 0
    even_x = lax.axis_index("gx") % 2 == 0
    even_y = lax.axis_index("gy") % 2 == 0
    for f, field in enumerate(fields):
        field_ref[f * levels : (f + 1) * levels, :] = field
        rim = PLANES[f] * plane
        low, high = field[:rim], field[levels - rim :]
        inner_x_ref[start : start + rim, :] = jnp.where(even_x, high, low)
        outer_x_ref[start : start + rim, :] = jnp.where(even_x, low, high)
        start += rim
    turned = jnp.concatenate(fields, axis=0).T
    low, high = turned[:WIDTH], turned[lanes - WIDTH :]
    inner_y_ref[...] = jnp.where(even_y, high, low)
    outer_y_ref[...] = jnp.where(even_y, low, high)


def deposit(incoming, fluid_mass, fluid_momentum):
    levels, lanes = fluid_mass.shape
    shapes = [(4 * levels, lanes)] + [(WIDTH, lanes)] * 2 + [(sum(PLANES) * 4, lanes)] * 2
    vmem = pl.BlockSpec(memory_space=pltpu.MemorySpace.VMEM)
    return pl.pallas_call(
        deposit_kernel,
        out_shape=tuple(jax.ShapeDtypeStruct(shape, jnp.float32) for shape in shapes),
        in_specs=[vmem] * 3,
        scratch_shapes=[
            pltpu.VMEM((4 * HIGH * LOW // lanes, lanes), jnp.float32),
            pltpu.VMEM((8 * HIGH, LOW), jnp.float32),
            pltpu.VMEM((2, 4 * HIGH, lanes), jnp.float32),
        ],
        compiler_params=pltpu.CompilerParams(vmem_limit_bytes=36 << 20),
        name="deposit",
    )(incoming, fluid_mass, fluid_momentum)


def swaps(axis, outer, sizes):
    pairs = []
    for x in range(sizes[0]):
        for y in range(sizes[1]):
            here = [x, y]
            there = here[axis] + (1 if (here[axis] % 2 == 0) != outer else -1)
            if 0 <= there < sizes[axis]:
                here[axis] = there
            else:
                here[1 - axis] ^= 1
            pairs.append((x * sizes[1] + y, here[0] * sizes[1] + here[1]))
    return pairs


def solve_kernel(sizes, field_ref, inner_y_ref, outer_y_ref, inner_x_ref, outer_x_ref, inner_c_ref, outer_c_ref, vel_ref, out_ref, sem):
    copy = pltpu.make_async_copy(field_ref.at[: vel_ref.shape[0]], vel_ref, sem)
    copy.start()
    depth = 4
    lanes = out_ref.shape[1]
    levels = out_ref.shape[0]
    rim = WIDTH * depth
    zero = jnp.zeros((lanes - 2 * WIDTH, lanes), jnp.float32)

    x, y = lax.axis_index("gx"), lax.axis_index("gy")
    even_x, even_y = x % 2 == 0, y % 2 == 0
    has_below, has_above = x > 0, x < sizes[0] - 1
    has_left, has_right = y > 0, y < sizes[1] - 1

    def sidewise(inner, outer):
        right = jnp.where(has_right, jnp.where(even_y, inner, outer), 0.0)
        left = jnp.where(has_left, jnp.where(even_y, outer, inner), 0.0)
        return jnp.concatenate([right, zero, left], axis=0).T

    inner_x, outer_x = inner_x_ref[...], outer_x_ref[...]
    below = jnp.where(has_below, jnp.where(even_x, outer_x, inner_x), 0.0)
    above = jnp.where(has_above, jnp.where(even_x, inner_x, outer_x), 0.0)
    inner_c, outer_c = inner_c_ref[...], outer_c_ref[...]
    below_c = jnp.where(has_below, jnp.where(even_x, outer_c, inner_c), 0.0)
    above_c = jnp.where(has_above, jnp.where(even_x, inner_c, outer_c), 0.0)
    own_side = sidewise(inner_y_ref[...], outer_y_ref[...])
    below_side = sidewise(below_c[:WIDTH], below_c[WIDTH:])
    above_side = sidewise(above_c[:WIDTH], above_c[WIDTH:])
    wide = []
    start = 0
    for f in range(4):
        kept = PLANES[f] * depth
        rows = [field_ref[f * levels : (f + 1) * levels, :]]
        if kept < rim:
            gap = jnp.zeros((rim - kept, lanes), jnp.float32)
            rows = [gap, below[start : start + kept]] + rows + [above[start : start + kept], gap]
        else:
            rows = [below[start : start + kept]] + rows + [above[start : start + kept]]
        start += kept
        second = jnp.concatenate(
            [
                below_side[(f + 1) * levels - rim : (f + 1) * levels],
                own_side[f * levels : (f + 1) * levels],
                above_side[f * levels : f * levels + rim],
            ],
            axis=0,
        )
        wide.append(jnp.concatenate([jnp.concatenate(rows, axis=0), second], axis=1))
    u, v, w, stiffness = wide
    total_rows = levels + 2 * rim

    def roll_rows(value, amount):
        return pltpu.roll(value, amount % total_rows, 0)

    def roll_lanes(value, amount):
        return pltpu.roll(value, amount % (2 * lanes), 1)

    row = lax.broadcasted_iota(jnp.int32, (total_rows, 2 * lanes), 0)
    z = row % depth

    def above_z(value):
        return jnp.where(z == depth - 1, 0.0, roll_rows(value, -1))

    def below_z(value):
        return jnp.where(z == 0, 0.0, roll_rows(value, 1))

    lane = lax.broadcasted_iota(jnp.int32, (total_rows, 2 * lanes), 1)
    first_row, last_row = jnp.where(has_below, 0, rim), jnp.where(has_above, total_rows, rim + levels)
    last_lane = jnp.where(has_right, lanes + WIDTH, lanes)
    first_left = jnp.where(has_left, 2 * lanes - WIDTH, 2 * lanes)
    inside = (row >= first_row) & (row < last_row) & ((lane < last_lane) | (lane >= first_left))
    source = -0.5 * (
        (roll_rows(u, -depth) - roll_rows(u, depth))
        + (roll_lanes(v, -1) - roll_lanes(v, 1))
        + (above_z(w) - below_z(w))
    )
    source = jnp.where(inside, source, 0.0)
    theta = (eigen_high + eigen_low) / 2.0
    delta = (eigen_high - eigen_low) / 2.0
    sigma = theta / delta
    rho = 1.0 / sigma
    pressure = jnp.zeros_like(source)
    residual = source
    search = source / theta
    for sweep in range(SWEEPS):
        pressure = pressure + search
        if sweep + 1 < SWEEPS:
            beside = (
                roll_rows(search, -depth) + roll_rows(search, depth)
                + roll_lanes(search, -1) + roll_lanes(search, 1)
                + above_z(search) + below_z(search)
            )
            residual = residual - ((6.0 + stiffness) * search - beside)
            rho_new = 1.0 / (2.0 * sigma - rho)
            search = rho_new * rho * search + 2.0 * rho_new / delta * residual
            search = jnp.where(inside, search, 0.0)
            rho = rho_new
    out_ref[...] = pressure[rim : rim + levels, :lanes]
    copy.wait()


def local(destination, row_count, old_cell, new_cell, point_mass, point_vel, grid_delta, fluid_mass, fluid_momentum):
    rows, lanes = point_mass.shape
    across, depth, along = fluid_mass.shape
    levels = across * depth
    sizes = (lax.axis_size("gx"), lax.axis_size("gy"))
    owners = sizes[0] * sizes[1]
    outgoing = pack(
        destination.reshape(1, rows),
        row_count.reshape(1, rows),
        old_cell,
        new_cell,
        point_mass,
        jnp.swapaxes(point_vel, 0, 1),
        grid_delta.reshape(3 * levels, along),
    )
    incoming = lax.all_to_all(
        outgoing.reshape(owners, 1, CAP * FIELDS * lanes), ("gx", "gy"), split_axis=0, concat_axis=0, tiled=True
    ).reshape(owners * CAP * FIELDS, lanes)
    fields, inner_y, outer_y, inner_x, outer_x = deposit(
        incoming, fluid_mass.reshape(levels, along), fluid_momentum.reshape(3 * levels, along)
    )

    def swap(value, axis, outer):
        return lax.ppermute(value, ("gx", "gy"), swaps(axis, outer, sizes))

    inner_y = swap(inner_y, 1, False)
    outer_y = swap(outer_y, 1, True)
    inner_x = swap(inner_x, 0, False)
    outer_x = swap(outer_x, 0, True)
    columns = jnp.concatenate([inner_y, outer_y], axis=0)
    inner_c = swap(columns, 0, False)
    outer_c = swap(columns, 0, True)
    vmem = pl.BlockSpec(memory_space=pltpu.MemorySpace.VMEM)
    velocity, pressure = pl.pallas_call(
        functools.partial(solve_kernel, sizes),
        out_shape=(
            jax.ShapeDtypeStruct((3 * levels, along), jnp.float32),
            jax.ShapeDtypeStruct((levels, along), jnp.float32),
        ),
        in_specs=[vmem] * 7,
        out_specs=(pl.BlockSpec(memory_space=pltpu.MemorySpace.HBM), vmem),
        scratch_shapes=[pltpu.SemaphoreType.DMA],
        compiler_params=pltpu.CompilerParams(vmem_limit_bytes=8 << 20),
        name="solve",
    )(fields, inner_y, outer_y, inner_x, outer_x, inner_c, outer_c)
    return velocity.reshape(3, across, depth, along), pressure.reshape(across, depth, along)


def solution(mesh):
    return jax.shard_map(
        local,
        mesh=mesh,
        in_specs=(
            P(("gx", "gy"), None),
            P(("gx", "gy")),
            P(("gx", "gy"), None),
            P(("gx", "gy"), None),
            P(("gx", "gy"), None),
            P(("gx", "gy"), None, None),
            P(None, "gx", None, "gy"),
            P("gx", None, "gy"),
            P(None, "gx", None, "gy"),
        ),
        out_specs=(P(None, "gx", None, "gy"), P("gx", None, "gy")),
        check_vma=False,
    )
```

```python
import functools

import jax
import jax.numpy as jnp
from jax import lax
from jax.experimental import pallas as pl
from jax.experimental.pallas import tpu as pltpu
from jax.sharding import PartitionSpec as P

CAP = 3
FIELDS = 5
SWEEPS = 4
WIDTH = 4
PLANES = (4, 3, 3, 2)
HIGH = 24
LOW = 192
GROUP = 64

eigen_low = 0.5
eigen_high = 14.5


def pieces(value):
    top = value.astype(jnp.bfloat16)
    return top, (value - top.astype(jnp.float32)).astype(jnp.bfloat16)


def pair_table(delta_ref):
    levels = delta_ref.shape[0] // 3
    tops, rests = [], []
    for c in range(3):
        halves = [delta_ref[pl.ds(c * levels + b, levels // 2, stride=2), :] for b in range(2)]
        top, rest = pieces(jnp.concatenate(halves, axis=1))
        tops.append(top)
        rests.append(rest)
    return jnp.concatenate(tops + rests, axis=0)


def collector(levels, count):
    half = levels // 2
    shape = (3 * count, count * 6 * half)
    out = lax.broadcasted_iota(jnp.int32, shape, 0)
    inner = lax.broadcasted_iota(jnp.int32, shape, 1)
    same = (inner // (6 * half) == out % count) & ((inner // half) % 3 == out // count)
    return jnp.where(same, 1.0, 0.0).astype(jnp.bfloat16)


def product_lookup(cells, table_ref, collect_ref):
    rows, lanes = cells.shape
    half = table_ref.shape[0] // 6
    spot = (cells & (2 * lanes - 1)).astype(jnp.float32)
    level = (cells >> 8).astype(jnp.float32)
    spot_index = row_index((2 * lanes, lanes))
    level_index = row_index((half, lanes))
    one, zero = whole((2 * lanes, lanes), 1.0), whole((2 * lanes, lanes), 0.0)

    def spread(values, r, height):
        return jnp.broadcast_to(values[r : r + 1, :], (height, lanes)).astype(jnp.bfloat16)

    hots = [jnp.where(spread(spot, r, 2 * lanes) == spot_index, one, zero) for r in range(rows)]
    blocks = []
    for r in range(0, rows, 2):
        looked = jnp.dot(
            table_ref[...], jnp.concatenate(hots[r : r + 2], axis=1), preferred_element_type=jnp.float32
        ).astype(jnp.bfloat16)
        for k in range(2):
            here = spread(level, r + k, half) == level_index
            for q in range(6):
                part = looked[q * half : (q + 1) * half, k * lanes : (k + 1) * lanes]
                blocks.append(jnp.where(here, part, whole((half, lanes), 0.0)))
    found = jnp.dot(collect_ref[...], jnp.concatenate(blocks, axis=0), preferred_element_type=jnp.float32)
    return [found[c * rows : (c + 1) * rows] for c in range(3)]


def lane_lookup(cell, delta_ref):
    step, lanes = cell.shape
    levels = delta_ref.shape[0] // 3
    along = cell & (lanes - 1)
    level = cell >> 7
    found = [jnp.zeros((step, lanes), jnp.float32)] * 3
    for c in range(3):
        for h in range(levels):
            table = jnp.broadcast_to(delta_ref[c * levels + h : c * levels + h + 1, :], (step, lanes))
            found[c] = jnp.where(level == h, jnp.take_along_axis(table, along, axis=1), found[c])
    return found


def pack_kernel(*refs):
    inputs, out_ref, staged, (live_ref, pay_ref, table_ref, collect_ref, sem) = (
        refs[:7],
        refs[7],
        refs[8:15],
        refs[15:],
    )
    copies = [pltpu.make_async_copy(src, dst, sem.at[i]) for i, (src, dst) in enumerate(zip(inputs, staged))]
    for copy in copies:
        copy.start()
    target_ref, count_ref, old_ref, new_ref, mass_ref, vel_ref, delta_ref = staged
    rows, lanes = mass_ref.shape
    owners = out_ref.shape[0] // (CAP * FIELDS)
    levels = delta_ref.shape[0] // 3
    copies[0].wait()
    target = jnp.broadcast_to(target_ref[...], (owners, rows))
    marks = target == lax.broadcasted_iota(jnp.int32, (owners, rows), 0)
    before = lax.broadcasted_iota(jnp.int32, (rows, rows), 0) < lax.broadcasted_iota(jnp.int32, (rows, rows), 1)
    ones = jnp.where(marks, 1.0, 0.0)
    earlier = jnp.dot(
        ones.astype(jnp.bfloat16), jnp.where(before, 1.0, 0.0).astype(jnp.bfloat16), preferred_element_type=jnp.float32
    )
    for copy in copies[1:]:
        copy.wait()
    lane_index = lax.broadcasted_iota(jnp.int32, (lanes, lanes), 1).astype(jnp.float32)
    for part in range(rows // lanes):
        band = slice(part * lanes, (part + 1) * lanes)
        counts = jnp.broadcast_to(count_ref[:, band].astype(jnp.float32), (lanes, lanes)).T
        live_ref[band, :] = jnp.where(lane_index < counts, mass_ref[band, :], 0.0)
    step = 16
    table_ref[...] = pair_table(delta_ref)
    collect_ref[...] = collector(levels, step // 2)

    def put(start, cell, found):
        band = pl.ds(pl.multiple_of(start, step), step)
        mass = live_ref[band, :]
        parts = [mass] + [mass * (vel_ref[c, band, :] + found[c]) for c in range(3)]
        parts.append(new_ref[band, :].astype(jnp.float32))
        for f, part in enumerate(parts):
            for k, piece in enumerate(pieces(part)):
                pay_ref[pl.ds(pl.multiple_of(k * rows + start, step), step), f * lanes : (f + 1) * lanes] = piece

    def lookup(start, by_lanes):
        cell = old_ref[pl.ds(pl.multiple_of(start, step), step), :]
        if by_lanes:
            found = lane_lookup(cell, delta_ref)
        else:
            upper, lower = (product_lookup(cell[h : h + step // 2], table_ref, collect_ref) for h in (0, step // 2))
            found = [jnp.concatenate(pair, axis=0) for pair in zip(upper, lower)]
        put(start, cell, found)

    per = 3 * step
    count = rows // per

    def gather(index, carry):
        lookup(index * per + 2 * step, False)
        for k in range(2):
            lookup(index * per + k * step, True)
        return carry

    lax.fori_loop(0, count, gather, 0)
    for start in range(count * per, rows, step):
        lookup(start, True)
    for s in range(CAP):
        chosen = jnp.where(earlier == float(s), ones, 0.0).astype(jnp.bfloat16)
        picked = jnp.dot(jnp.concatenate([chosen] * 2, axis=1), pay_ref[...], preferred_element_type=jnp.float32)
        for f in range(FIELDS):
            out_ref[pl.ds(f * CAP + s, owners, stride=CAP * FIELDS), :] = picked[:, f * lanes : (f + 1) * lanes]


def pack(*args):
    rows, lanes = args[4].shape
    owners = lax.axis_size("gx") * lax.axis_size("gy")
    return pl.pallas_call(
        pack_kernel,
        out_shape=jax.ShapeDtypeStruct((owners * CAP * FIELDS, lanes), jnp.float32),
        in_specs=[pl.BlockSpec(memory_space=pltpu.MemorySpace.HBM)] * len(args),
        scratch_shapes=[pltpu.VMEM(a.shape, a.dtype) for a in args]
        + [
            pltpu.VMEM((rows, lanes), jnp.float32),
            pltpu.VMEM((2 * rows, FIELDS * lanes), jnp.bfloat16),
            pltpu.VMEM((args[6].shape[0], 2 * lanes), jnp.bfloat16),
            pltpu.VMEM((24, 8 * args[6].shape[0]), jnp.bfloat16),
            pltpu.SemaphoreType.DMA((len(args),)),
        ],
        compiler_params=pltpu.CompilerParams(vmem_limit_bytes=16 << 20),
        name="pack",
    )(*[pltpu.with_memory_space_constraint(a, pltpu.MemorySpace.HBM) for a in args])


def whole(shape, value):
    return jnp.full(shape, value, jnp.bfloat16)


def row_index(shape):
    return lax.broadcasted_iota(jnp.int32, shape, 0).astype(jnp.float32).astype(jnp.bfloat16)


def deposit_kernel(in_ref, mass_ref, momentum_ref, field_ref, *rest):
    acc_ref, turn_ref = rest[-2:]
    lanes = in_ref.shape[1]
    sources = in_ref.shape[0] // (CAP * FIELDS)
    group = GROUP
    acc_ref[...] = jnp.zeros_like(acc_ref)
    low_index = row_index((LOW, lanes))
    high_index = jnp.concatenate([lax.broadcasted_iota(jnp.int32, (HIGH, lanes), 0)] * 2, axis=0)
    high_index = high_index.astype(jnp.float32).astype(jnp.bfloat16)
    one, zero = whole((LOW, lanes), 1.0), whole((LOW, lanes), 0.0)
    nothing = whole((2 * HIGH, lanes), 0.0)

    def add(index, carry):
        lefts, rights = [], []
        for g in range(group):
            base = (index * group + g) * (CAP * FIELDS)
            for s in range(CAP):
                row = lambda f: in_ref[pl.ds(base + f * CAP + s, 1), :]
                cell = row(4).astype(jnp.int32)
                high = ((cell >> 6) * 171) >> 9
                low = (cell - high * LOW).astype(jnp.float32)
                low = jnp.broadcast_to(low, (LOW, lanes)).astype(jnp.bfloat16)
                high = jnp.broadcast_to(high.astype(jnp.float32), (2 * HIGH, lanes)).astype(jnp.bfloat16)
                lefts.append(jnp.where(low == low_index, one, zero))
                here = high == high_index
                for c in range(4):
                    value = row(c)
                    top = value.astype(jnp.bfloat16).astype(jnp.float32)
                    both = [jnp.broadcast_to(piece, (HIGH, lanes)) for piece in (top, value - top)]
                    rights.append(jnp.where(here, jnp.concatenate(both, axis=0).astype(jnp.bfloat16), nothing))
        left = jnp.concatenate(lefts, axis=1)
        right = jnp.concatenate(
            [jnp.concatenate(rights[4 * i : 4 * i + 4], axis=0) for i in range(len(lefts))], axis=1
        )
        acc_ref[...] += lax.dot_general(right, left, (((1,), (1,)), ((), ())), preferred_element_type=jnp.float32)
        return carry

    lax.fori_loop(0, sources // group, add, 0)
    for c in range(4):
        part = acc_ref[2 * c * HIGH : (2 * c + 1) * HIGH, :] + acc_ref[(2 * c + 1) * HIGH : (2 * c + 2) * HIGH, :]
        turn_ref[0, c * HIGH : (c + 1) * HIGH, :] = part[:, :lanes]
        turn_ref[1, c * HIGH : (c + 1) * HIGH, : LOW - lanes] = part[:, lanes:]
    pairs = 2 * HIGH
    half = lanes // 2
    even, odd = pl.ds(0, pairs, stride=2), pl.ds(1, pairs, stride=2)
    cells_ref = rest[-3]
    cells_ref[pl.ds(0, pairs, stride=3), :] = turn_ref[0, even, :]
    odd_row = turn_ref[0, odd, :]
    cells_ref[pl.ds(1, pairs, stride=3), :] = jnp.concatenate([turn_ref[1, even, :][:, :half], odd_row[:, :half]], axis=1)
    cells_ref[pl.ds(2, pairs, stride=3), :] = jnp.concatenate([odd_row[:, half:], turn_ref[1, odd, :][:, :half]], axis=1)
    levels = mass_ref.shape[0]
    span = HIGH * LOW // lanes
    sums = [cells_ref[c * span : c * span + levels, :] for c in range(4)]
    finish(sums, mass_ref, momentum_ref, field_ref, *rest[:-3])


def finish(sums, mass_ref, momentum_ref, field_ref, inner_y_ref, outer_y_ref, inner_x_ref, outer_x_ref):
    levels, lanes = mass_ref.shape
    total = mass_ref[...] + sums[0]
    fields = [
        (momentum_ref[c * levels : (c + 1) * levels, :] + sums[c + 1]) / total
        for c in range(3)
    ]
    fields.append(0.5 + 1.0 / total)
    plane = inner_x_ref.shape[0] // sum(PLANES)
    start = 0
    even_x = lax.axis_index("gx") % 2 == 0
    even_y = lax.axis_index("gy") % 2 == 0
    for f, field in enumerate(fields):
        field_ref[f * levels : (f + 1) * levels, :] = field
        rim = PLANES[f] * plane
        low, high = field[:rim], field[levels - rim :]
        inner_x_ref[start : start + rim, :] = jnp.where(even_x, high, low)
        outer_x_ref[start : start + rim, :] = jnp.where(even_x, low, high)
        start += rim
    turned = jnp.concatenate(fields, axis=0).T
    low, high = turned[:WIDTH], turned[lanes - WIDTH :]
    inner_y_ref[...] = jnp.where(even_y, high, low)
    outer_y_ref[...] = jnp.where(even_y, low, high)


def deposit(incoming, fluid_mass, fluid_momentum):
    levels, lanes = fluid_mass.shape
    shapes = [(4 * levels, lanes)] + [(WIDTH, lanes)] * 2 + [(sum(PLANES) * 4, lanes)] * 2
    vmem = pl.BlockSpec(memory_space=pltpu.MemorySpace.VMEM)
    return pl.pallas_call(
        deposit_kernel,
        out_shape=tuple(jax.ShapeDtypeStruct(shape, jnp.float32) for shape in shapes),
        in_specs=[vmem] * 3,
        scratch_shapes=[
            pltpu.VMEM((4 * HIGH * LOW // lanes, lanes), jnp.float32),
            pltpu.VMEM((8 * HIGH, LOW), jnp.float32),
            pltpu.VMEM((2, 4 * HIGH, lanes), jnp.float32),
        ],
        compiler_params=pltpu.CompilerParams(vmem_limit_bytes=36 << 20),
        name="deposit",
    )(incoming, fluid_mass, fluid_momentum)


def swaps(axis, outer, sizes):
    pairs = []
    for x in range(sizes[0]):
        for y in range(sizes[1]):
            here = [x, y]
            there = here[axis] + (1 if (here[axis] % 2 == 0) != outer else -1)
            if 0 <= there < sizes[axis]:
                here[axis] = there
            else:
                here[1 - axis] ^= 1
            pairs.append((x * sizes[1] + y, here[0] * sizes[1] + here[1]))
    return pairs


def solve_kernel(sizes, field_ref, inner_y_ref, outer_y_ref, inner_x_ref, outer_x_ref, inner_c_ref, outer_c_ref, vel_ref, out_ref, sem):
    copy = pltpu.make_async_copy(field_ref.at[: vel_ref.shape[0]], vel_ref, sem)
    copy.start()
    depth = 4
    lanes = out_ref.shape[1]
    levels = out_ref.shape[0]
    rim = WIDTH * depth
    zero = jnp.zeros((lanes - 2 * WIDTH, lanes), jnp.float32)

    x, y = lax.axis_index("gx"), lax.axis_index("gy")
    even_x, even_y = x % 2 == 0, y % 2 == 0
    has_below, has_above = x > 0, x < sizes[0] - 1
    has_left, has_right = y > 0, y < sizes[1] - 1

    def sidewise(inner, outer):
        right = jnp.where(has_right, jnp.where(even_y, inner, outer), 0.0)
        left = jnp.where(has_left, jnp.where(even_y, outer, inner), 0.0)
        return jnp.concatenate([right, zero, left], axis=0).T

    inner_x, outer_x = inner_x_ref[...], outer_x_ref[...]
    below = jnp.where(has_below, jnp.where(even_x, outer_x, inner_x), 0.0)
    above = jnp.where(has_above, jnp.where(even_x, inner_x, outer_x), 0.0)
    inner_c, outer_c = inner_c_ref[...], outer_c_ref[...]
    below_c = jnp.where(has_below, jnp.where(even_x, outer_c, inner_c), 0.0)
    above_c = jnp.where(has_above, jnp.where(even_x, inner_c, outer_c), 0.0)
    own_side = sidewise(inner_y_ref[...], outer_y_ref[...])
    below_side = sidewise(below_c[:WIDTH], below_c[WIDTH:])
    above_side = sidewise(above_c[:WIDTH], above_c[WIDTH:])
    wide = []
    start = 0
    for f in range(4):
        kept = PLANES[f] * depth
        rows = [field_ref[f * levels : (f + 1) * levels, :]]
        if kept < rim:
            gap = jnp.zeros((rim - kept, lanes), jnp.float32)
            rows = [gap, below[start : start + kept]] + rows + [above[start : start + kept], gap]
        else:
            rows = [below[start : start + kept]] + rows + [above[start : start + kept]]
        start += kept
        second = jnp.concatenate(
            [
                below_side[(f + 1) * levels - rim : (f + 1) * levels],
                own_side[f * levels : (f + 1) * levels],
                above_side[f * levels : f * levels + rim],
            ],
            axis=0,
        )
        wide.append(jnp.concatenate([jnp.concatenate(rows, axis=0), second], axis=1))
    u, v, w, stiffness = wide
    total_rows = levels + 2 * rim

    def roll_rows(value, amount):
        return pltpu.roll(value, amount % total_rows, 0)

    def roll_lanes(value, amount):
        return pltpu.roll(value, amount % (2 * lanes), 1)

    row = lax.broadcasted_iota(jnp.int32, (total_rows, 2 * lanes), 0)
    z = row % depth

    def above_z(value):
        return jnp.where(z == depth - 1, 0.0, roll_rows(value, -1))

    def below_z(value):
        return jnp.where(z == 0, 0.0, roll_rows(value, 1))

    lane = lax.broadcasted_iota(jnp.int32, (total_rows, 2 * lanes), 1)
    first_row, last_row = jnp.where(has_below, 0, rim), jnp.where(has_above, total_rows, rim + levels)
    last_lane = jnp.where(has_right, lanes + WIDTH, lanes)
    first_left = jnp.where(has_left, 2 * lanes - WIDTH, 2 * lanes)
    inside = (row >= first_row) & (row < last_row) & ((lane < last_lane) | (lane >= first_left))
    source = -0.5 * (
        (roll_rows(u, -depth) - roll_rows(u, depth))
        + (roll_lanes(v, -1) - roll_lanes(v, 1))
        + (above_z(w) - below_z(w))
    )
    source = jnp.where(inside, source, 0.0)
    theta = (eigen_high + eigen_low) / 2.0
    delta = (eigen_high - eigen_low) / 2.0
    sigma = theta / delta
    rho = 1.0 / sigma
    pressure = jnp.zeros_like(source)
    residual = source
    search = source / theta
    for sweep in range(SWEEPS):
        pressure = pressure + search
        if sweep + 1 < SWEEPS:
            beside = (
                roll_rows(search, -depth) + roll_rows(search, depth)
                + roll_lanes(search, -1) + roll_lanes(search, 1)
                + above_z(search) + below_z(search)
            )
            residual = residual - ((6.0 + stiffness) * search - beside)
            rho_new = 1.0 / (2.0 * sigma - rho)
            search = rho_new * rho * search + 2.0 * rho_new / delta * residual
            search = jnp.where(inside, search, 0.0)
            rho = rho_new
    out_ref[...] = pressure[rim : rim + levels, :lanes]
    copy.wait()


def local(destination, row_count, old_cell, new_cell, point_mass, point_vel, grid_delta, fluid_mass, fluid_momentum):
    rows, lanes = point_mass.shape
    across, depth, along = fluid_mass.shape
    levels = across * depth
    sizes = (lax.axis_size("gx"), lax.axis_size("gy"))
    owners = sizes[0] * sizes[1]
    outgoing = pack(
        destination.reshape(1, rows),
        row_count.reshape(1, rows),
        old_cell,
        new_cell,
        point_mass,
        jnp.swapaxes(point_vel, 0, 1),
        grid_delta.reshape(3 * levels, along),
    )
    incoming = lax.all_to_all(
        outgoing.reshape(owners, 1, CAP * FIELDS * lanes), ("gx", "gy"), split_axis=0, concat_axis=0, tiled=True
    ).reshape(owners * CAP * FIELDS, lanes)
    fields, inner_y, outer_y, inner_x, outer_x = deposit(
        incoming, fluid_mass.reshape(levels, along), fluid_momentum.reshape(3 * levels, along)
    )

    def swap(value, axis, outer):
        return lax.ppermute(value, ("gx", "gy"), swaps(axis, outer, sizes))

    inner_y = swap(inner_y, 1, False)
    outer_y = swap(outer_y, 1, True)
    inner_x = swap(inner_x, 0, False)
    outer_x = swap(outer_x, 0, True)
    columns = jnp.concatenate([inner_y, outer_y], axis=0)
    inner_c = swap(columns, 0, False)
    outer_c = swap(columns, 0, True)
    vmem = pl.BlockSpec(memory_space=pltpu.MemorySpace.VMEM)
    velocity, pressure = pl.pallas_call(
        functools.partial(solve_kernel, sizes),
        out_shape=(
            jax.ShapeDtypeStruct((3 * levels, along), jnp.float32),
            jax.ShapeDtypeStruct((levels, along), jnp.float32),
        ),
        in_specs=[vmem] * 7,
        out_specs=(pl.BlockSpec(memory_space=pltpu.MemorySpace.HBM), vmem),
        scratch_shapes=[pltpu.SemaphoreType.DMA],
        compiler_params=pltpu.CompilerParams(vmem_limit_bytes=8 << 20),
        name="solve",
    )(fields, inner_y, outer_y, inner_x, outer_x, inner_c, outer_c)
    return velocity.reshape(3, across, depth, along), pressure.reshape(across, depth, along)


def solution(mesh):
    return jax.shard_map(
        local,
        mesh=mesh,
        in_specs=(
            P(("gx", "gy"), None),
            P(("gx", "gy")),
            P(("gx", "gy"), None),
            P(("gx", "gy"), None),
            P(("gx", "gy"), None),
            P(("gx", "gy"), None, None),
            P(None, "gx", None, "gy"),
            P("gx", None, "gy"),
            P(None, "gx", None, "gy"),
        ),
        out_specs=(P(None, "gx", None, "gy"), P("gx", None, "gy")),
        check_vma=False,
    )
```

```python
import functools

import jax
import jax.numpy as jnp
from jax import lax
from jax.experimental import pallas as pl
from jax.experimental.pallas import tpu as pltpu
from jax.sharding import PartitionSpec as P

CAP = 3
FIELDS = 5
SWEEPS = 4
WIDTH = 4
PLANES = (4, 3, 3, 2)
HIGH = 24
LOW = 192
GROUP = 128

eigen_low = 0.5
eigen_high = 14.5


def pieces(value):
    top = value.astype(jnp.bfloat16)
    return top, (value - top.astype(jnp.float32)).astype(jnp.bfloat16)


def pair_table(delta_ref):
    levels = delta_ref.shape[0] // 3
    tops, rests = [], []
    for c in range(3):
        halves = [delta_ref[pl.ds(c * levels + b, levels // 2, stride=2), :] for b in range(2)]
        top, rest = pieces(jnp.concatenate(halves, axis=1))
        tops.append(top)
        rests.append(rest)
    return jnp.concatenate(tops + rests, axis=0)


def collector(levels, count):
    half = levels // 2
    shape = (3 * count, count * 6 * half)
    out = lax.broadcasted_iota(jnp.int32, shape, 0)
    inner = lax.broadcasted_iota(jnp.int32, shape, 1)
    same = (inner // (6 * half) == out % count) & ((inner // half) % 3 == out // count)
    return jnp.where(same, 1.0, 0.0).astype(jnp.bfloat16)


def product_lookup(cells, table_ref, collect_ref):
    rows, lanes = cells.shape
    half = table_ref.shape[0] // 6
    spot = (cells & (2 * lanes - 1)).astype(jnp.float32)
    level = (cells >> 8).astype(jnp.float32)
    spot_index = row_index((2 * lanes, lanes))
    level_index = row_index((half, lanes))
    one, zero = whole((2 * lanes, lanes), 1.0), whole((2 * lanes, lanes), 0.0)

    def spread(values, r, height):
        return jnp.broadcast_to(values[r : r + 1, :], (height, lanes)).astype(jnp.bfloat16)

    hots = [jnp.where(spread(spot, r, 2 * lanes) == spot_index, one, zero) for r in range(rows)]
    blocks = []
    for r in range(0, rows, 2):
        looked = jnp.dot(
            table_ref[...], jnp.concatenate(hots[r : r + 2], axis=1), preferred_element_type=jnp.float32
        ).astype(jnp.bfloat16)
        for k in range(2):
            here = spread(level, r + k, half) == level_index
            for q in range(6):
                part = looked[q * half : (q + 1) * half, k * lanes : (k + 1) * lanes]
                blocks.append(jnp.where(here, part, whole((half, lanes), 0.0)))
    found = jnp.dot(collect_ref[...], jnp.concatenate(blocks, axis=0), preferred_element_type=jnp.float32)
    return [found[c * rows : (c + 1) * rows] for c in range(3)]


def lane_lookup(cell, delta_ref):
    step, lanes = cell.shape
    levels = delta_ref.shape[0] // 3
    along = cell & (lanes - 1)
    level = cell >> 7
    found = [jnp.zeros((step, lanes), jnp.float32)] * 3
    for c in range(3):
        for h in range(levels):
            table = jnp.broadcast_to(delta_ref[c * levels + h : c * levels + h + 1, :], (step, lanes))
            found[c] = jnp.where(level == h, jnp.take_along_axis(table, along, axis=1), found[c])
    return found


def pack_kernel(*refs):
    inputs, out_ref, staged, (live_ref, pay_ref, table_ref, collect_ref, sem) = (
        refs[:7],
        refs[7],
        refs[8:15],
        refs[15:],
    )
    copies = [pltpu.make_async_copy(src, dst, sem.at[i]) for i, (src, dst) in enumerate(zip(inputs, staged))]
    for copy in copies:
        copy.start()
    target_ref, count_ref, old_ref, new_ref, mass_ref, vel_ref, delta_ref = staged
    rows, lanes = mass_ref.shape
    owners = out_ref.shape[0] // (CAP * FIELDS)
    levels = delta_ref.shape[0] // 3
    step = 16
    collect_ref[...] = collector(levels, step // 2)
    copies[0].wait()
    target = jnp.broadcast_to(target_ref[...], (owners, rows))
    marks = target == lax.broadcasted_iota(jnp.int32, (owners, rows), 0)
    before = lax.broadcasted_iota(jnp.int32, (rows, rows), 0) < lax.broadcasted_iota(jnp.int32, (rows, rows), 1)
    ones = jnp.where(marks, 1.0, 0.0)
    earlier = jnp.dot(
        ones.astype(jnp.bfloat16), jnp.where(before, 1.0, 0.0).astype(jnp.bfloat16), preferred_element_type=jnp.float32
    )
    copies[6].wait()
    table_ref[...] = pair_table(delta_ref)
    for copy in copies[1:6]:
        copy.wait()
    lane_index = lax.broadcasted_iota(jnp.int32, (lanes, lanes), 1).astype(jnp.float32)
    for part in range(rows // lanes):
        band = slice(part * lanes, (part + 1) * lanes)
        counts = jnp.broadcast_to(count_ref[:, band].astype(jnp.float32), (lanes, lanes)).T
        live_ref[band, :] = jnp.where(lane_index < counts, mass_ref[band, :], 0.0)
    def put(start, cell, found):
        band = pl.ds(pl.multiple_of(start, step), step)
        mass = live_ref[band, :]
        parts = [mass] + [mass * (vel_ref[c, band, :] + found[c]) for c in range(3)]
        parts.append(new_ref[band, :].astype(jnp.float32))
        for f, part in enumerate(parts):
            for k, piece in enumerate(pieces(part)):
                pay_ref[pl.ds(pl.multiple_of(k * rows + start, step), step), f * lanes : (f + 1) * lanes] = piece

    def lookup(start, by_lanes):
        cell = old_ref[pl.ds(pl.multiple_of(start, step), step), :]
        if by_lanes:
            found = lane_lookup(cell, delta_ref)
        else:
            upper, lower = (product_lookup(cell[h : h + step // 2], table_ref, collect_ref) for h in (0, step // 2))
            found = [jnp.concatenate(pair, axis=0) for pair in zip(upper, lower)]
        put(start, cell, found)

    per = 3 * step
    count = rows // per

    def gather(index, carry):
        lookup(index * per + 2 * step, False)
        for k in range(2):
            lookup(index * per + k * step, True)
        return carry

    lax.fori_loop(0, count, gather, 0)
    for start in range(count * per, rows, step):
        lookup(start, True)
    chosen = jnp.concatenate([jnp.where(earlier == float(s), ones, 0.0) for s in range(CAP)], axis=0).astype(jnp.bfloat16)
    picked = jnp.dot(jnp.concatenate([chosen] * 2, axis=1), pay_ref[...], preferred_element_type=jnp.float32)
    for s in range(CAP):
        for f in range(FIELDS):
            part = picked[s * owners : (s + 1) * owners, f * lanes : (f + 1) * lanes]
            out_ref[pl.ds(f * CAP + s, owners, stride=CAP * FIELDS), :] = part


def pack(*args):
    rows, lanes = args[4].shape
    owners = lax.axis_size("gx") * lax.axis_size("gy")
    return pl.pallas_call(
        pack_kernel,
        out_shape=jax.ShapeDtypeStruct((owners * CAP * FIELDS, lanes), jnp.float32),
        in_specs=[pl.BlockSpec(memory_space=pltpu.MemorySpace.HBM)] * len(args),
        scratch_shapes=[pltpu.VMEM(a.shape, a.dtype) for a in args]
        + [
            pltpu.VMEM((rows, lanes), jnp.float32),
            pltpu.VMEM((2 * rows, FIELDS * lanes), jnp.bfloat16),
            pltpu.VMEM((args[6].shape[0], 2 * lanes), jnp.bfloat16),
            pltpu.VMEM((24, 8 * args[6].shape[0]), jnp.bfloat16),
            pltpu.SemaphoreType.DMA((len(args),)),
        ],
        compiler_params=pltpu.CompilerParams(vmem_limit_bytes=16 << 20),
        name="pack",
    )(*[pltpu.with_memory_space_constraint(a, pltpu.MemorySpace.HBM) for a in args])


def whole(shape, value):
    return jnp.full(shape, value, jnp.bfloat16)


def row_index(shape):
    return lax.broadcasted_iota(jnp.int32, shape, 0).astype(jnp.float32).astype(jnp.bfloat16)


def deposit_kernel(in_ref, mass_ref, momentum_ref, field_ref, *rest):
    acc_ref, turn_ref = rest[-2:]
    lanes = in_ref.shape[1]
    sources = in_ref.shape[0] // (CAP * FIELDS)
    group = GROUP
    acc_ref[...] = jnp.zeros_like(acc_ref)
    low_index = row_index((LOW, lanes))
    high_index = jnp.concatenate([lax.broadcasted_iota(jnp.int32, (HIGH, lanes), 0)] * 2, axis=0)
    high_index = high_index.astype(jnp.float32).astype(jnp.bfloat16)
    one, zero = whole((LOW, lanes), 1.0), whole((LOW, lanes), 0.0)
    nothing = whole((2 * HIGH, lanes), 0.0)

    def add(index, carry):
        lefts, rights = [], []
        for g in range(group):
            base = (index * group + g) * (CAP * FIELDS)
            for s in range(CAP):
                row = lambda f: in_ref[pl.ds(base + f * CAP + s, 1), :]
                cell = row(4).astype(jnp.int32)
                high = ((cell >> 6) * 171) >> 9
                low = (cell - high * LOW).astype(jnp.float32)
                low = jnp.broadcast_to(low, (LOW, lanes)).astype(jnp.bfloat16)
                high = jnp.broadcast_to(high.astype(jnp.float32), (2 * HIGH, lanes)).astype(jnp.bfloat16)
                lefts.append(jnp.where(low == low_index, one, zero))
                here = high == high_index
                for c in range(4):
                    value = row(c)
                    top = value.astype(jnp.bfloat16).astype(jnp.float32)
                    both = [jnp.broadcast_to(piece, (HIGH, lanes)) for piece in (top, value - top)]
                    rights.append(jnp.where(here, jnp.concatenate(both, axis=0).astype(jnp.bfloat16), nothing))
        left = jnp.concatenate(lefts, axis=1)
        right = jnp.concatenate(
            [jnp.concatenate(rights[4 * i : 4 * i + 4], axis=0) for i in range(len(lefts))], axis=1
        )
        acc_ref[...] += lax.dot_general(right, left, (((1,), (1,)), ((), ())), preferred_element_type=jnp.float32)
        return carry

    lax.fori_loop(0, sources // group, add, 0)
    for c in range(4):
        part = acc_ref[2 * c * HIGH : (2 * c + 1) * HIGH, :] + acc_ref[(2 * c + 1) * HIGH : (2 * c + 2) * HIGH, :]
        turn_ref[0, c * HIGH : (c + 1) * HIGH, :] = part[:, :lanes]
        turn_ref[1, c * HIGH : (c + 1) * HIGH, : LOW - lanes] = part[:, lanes:]
    pairs = 2 * HIGH
    half = lanes // 2
    even, odd = pl.ds(0, pairs, stride=2), pl.ds(1, pairs, stride=2)
    cells_ref = rest[-3]
    cells_ref[pl.ds(0, pairs, stride=3), :] = turn_ref[0, even, :]
    odd_row = turn_ref[0, odd, :]
    cells_ref[pl.ds(1, pairs, stride=3), :] = jnp.concatenate([turn_ref[1, even, :][:, :half], odd_row[:, :half]], axis=1)
    cells_ref[pl.ds(2, pairs, stride=3), :] = jnp.concatenate([odd_row[:, half:], turn_ref[1, odd, :][:, :half]], axis=1)
    levels = mass_ref.shape[0]
    span = HIGH * LOW // lanes
    sums = [cells_ref[c * span : c * span + levels, :] for c in range(4)]
    finish(sums, mass_ref, momentum_ref, field_ref, *rest[:-3])


def finish(sums, mass_ref, momentum_ref, field_ref, inner_y_ref, outer_y_ref, inner_x_ref, outer_x_ref):
    levels, lanes = mass_ref.shape
    total = mass_ref[...] + sums[0]
    fields = [
        (momentum_ref[c * levels : (c + 1) * levels, :] + sums[c + 1]) / total
        for c in range(3)
    ]
    fields.append(0.5 + 1.0 / total)
    plane = inner_x_ref.shape[0] // sum(PLANES)
    start = 0
    even_x = lax.axis_index("gx") % 2 == 0
    even_y = lax.axis_index("gy") % 2 == 0
    for f, field in enumerate(fields):
        field_ref[f * levels : (f + 1) * levels, :] = field
        rim = PLANES[f] * plane
        low, high = field[:rim], field[levels - rim :]
        inner_x_ref[start : start + rim, :] = jnp.where(even_x, high, low)
        outer_x_ref[start : start + rim, :] = jnp.where(even_x, low, high)
        start += rim
    turned = jnp.concatenate(fields, axis=0).T
    low, high = turned[:WIDTH], turned[lanes - WIDTH :]
    inner_y_ref[...] = jnp.where(even_y, high, low)
    outer_y_ref[...] = jnp.where(even_y, low, high)


def deposit(incoming, fluid_mass, fluid_momentum):
    levels, lanes = fluid_mass.shape
    shapes = [(4 * levels, lanes)] + [(WIDTH, lanes)] * 2 + [(sum(PLANES) * 4, lanes)] * 2
    vmem = pl.BlockSpec(memory_space=pltpu.MemorySpace.VMEM)
    return pl.pallas_call(
        deposit_kernel,
        out_shape=tuple(jax.ShapeDtypeStruct(shape, jnp.float32) for shape in shapes),
        in_specs=[vmem] * 3,
        scratch_shapes=[
            pltpu.VMEM((4 * HIGH * LOW // lanes, lanes), jnp.float32),
            pltpu.VMEM((8 * HIGH, LOW), jnp.float32),
            pltpu.VMEM((2, 4 * HIGH, lanes), jnp.float32),
        ],
        compiler_params=pltpu.CompilerParams(vmem_limit_bytes=50 << 20),
        name="deposit",
    )(incoming, fluid_mass, fluid_momentum)


def swaps(axis, outer, sizes):
    pairs = []
    for x in range(sizes[0]):
        for y in range(sizes[1]):
            here = [x, y]
            there = here[axis] + (1 if (here[axis] % 2 == 0) != outer else -1)
            if 0 <= there < sizes[axis]:
                here[axis] = there
            else:
                here[1 - axis] ^= 1
            pairs.append((x * sizes[1] + y, here[0] * sizes[1] + here[1]))
    return pairs


def solve_kernel(sizes, field_ref, inner_y_ref, outer_y_ref, inner_x_ref, outer_x_ref, inner_c_ref, outer_c_ref, vel_ref, out_ref, sem):
    copy = pltpu.make_async_copy(field_ref.at[: vel_ref.shape[0]], vel_ref, sem)
    copy.start()
    depth = 4
    lanes = out_ref.shape[1]
    levels = out_ref.shape[0]
    rim = WIDTH * depth
    zero = jnp.zeros((lanes - 2 * WIDTH, lanes), jnp.float32)

    x, y = lax.axis_index("gx"), lax.axis_index("gy")
    even_x, even_y = x % 2 == 0, y % 2 == 0
    has_below, has_above = x > 0, x < sizes[0] - 1
    has_left, has_right = y > 0, y < sizes[1] - 1

    def sidewise(inner, outer):
        right = jnp.where(has_right, jnp.where(even_y, inner, outer), 0.0)
        left = jnp.where(has_left, jnp.where(even_y, outer, inner), 0.0)
        return jnp.concatenate([right, zero, left], axis=0).T

    inner_x, outer_x = inner_x_ref[...], outer_x_ref[...]
    below = jnp.where(has_below, jnp.where(even_x, outer_x, inner_x), 0.0)
    above = jnp.where(has_above, jnp.where(even_x, inner_x, outer_x), 0.0)
    inner_c, outer_c = inner_c_ref[...], outer_c_ref[...]
    below_c = jnp.where(has_below, jnp.where(even_x, outer_c, inner_c), 0.0)
    above_c = jnp.where(has_above, jnp.where(even_x, inner_c, outer_c), 0.0)
    own_side = sidewise(inner_y_ref[...], outer_y_ref[...])
    below_side = sidewise(below_c[:WIDTH], below_c[WIDTH:])
    above_side = sidewise(above_c[:WIDTH], above_c[WIDTH:])
    wide = []
    start = 0
    for f in range(4):
        kept = PLANES[f] * depth
        rows = [field_ref[f * levels : (f + 1) * levels, :]]
        if kept < rim:
            gap = jnp.zeros((rim - kept, lanes), jnp.float32)
            rows = [gap, below[start : start + kept]] + rows + [above[start : start + kept], gap]
        else:
            rows = [below[start : start + kept]] + rows + [above[start : start + kept]]
        start += kept
        second = jnp.concatenate(
            [
                below_side[(f + 1) * levels - rim : (f + 1) * levels],
                own_side[f * levels : (f + 1) * levels],
                above_side[f * levels : f * levels + rim],
            ],
            axis=0,
        )
        wide.append(jnp.concatenate([jnp.concatenate(rows, axis=0), second], axis=1))
    u, v, w, stiffness = wide
    total_rows = levels + 2 * rim

    def roll_rows(value, amount):
        return pltpu.roll(value, amount % total_rows, 0)

    def roll_lanes(value, amount):
        return pltpu.roll(value, amount % (2 * lanes), 1)

    row = lax.broadcasted_iota(jnp.int32, (total_rows, 2 * lanes), 0)
    z = row % depth

    def above_z(value):
        return jnp.where(z == depth - 1, 0.0, roll_rows(value, -1))

    def below_z(value):
        return jnp.where(z == 0, 0.0, roll_rows(value, 1))

    lane = lax.broadcasted_iota(jnp.int32, (total_rows, 2 * lanes), 1)
    first_row, last_row = jnp.where(has_below, 0, rim), jnp.where(has_above, total_rows, rim + levels)
    last_lane = jnp.where(has_right, lanes + WIDTH, lanes)
    first_left = jnp.where(has_left, 2 * lanes - WIDTH, 2 * lanes)
    inside = (row >= first_row) & (row < last_row) & ((lane < last_lane) | (lane >= first_left))
    source = -0.5 * (
        (roll_rows(u, -depth) - roll_rows(u, depth))
        + (roll_lanes(v, -1) - roll_lanes(v, 1))
        + (above_z(w) - below_z(w))
    )
    source = jnp.where(inside, source, 0.0)
    theta = (eigen_high + eigen_low) / 2.0
    delta = (eigen_high - eigen_low) / 2.0
    sigma = theta / delta
    rho = 1.0 / sigma
    pressure = jnp.zeros_like(source)
    residual = source
    search = source / theta
    for sweep in range(SWEEPS):
        pressure = pressure + search
        if sweep + 1 < SWEEPS:
            beside = (
                roll_rows(search, -depth) + roll_rows(search, depth)
                + roll_lanes(search, -1) + roll_lanes(search, 1)
                + above_z(search) + below_z(search)
            )
            residual = residual - ((6.0 + stiffness) * search - beside)
            rho_new = 1.0 / (2.0 * sigma - rho)
            search = rho_new * rho * search + 2.0 * rho_new / delta * residual
            search = jnp.where(inside, search, 0.0)
            rho = rho_new
    out_ref[...] = pressure[rim : rim + levels, :lanes]
    copy.wait()


def local(destination, row_count, old_cell, new_cell, point_mass, point_vel, grid_delta, fluid_mass, fluid_momentum):
    rows, lanes = point_mass.shape
    across, depth, along = fluid_mass.shape
    levels = across * depth
    sizes = (lax.axis_size("gx"), lax.axis_size("gy"))
    owners = sizes[0] * sizes[1]
    outgoing = pack(
        destination.reshape(1, rows),
        row_count.reshape(1, rows),
        old_cell,
        new_cell,
        point_mass,
        jnp.swapaxes(point_vel, 0, 1),
        grid_delta.reshape(3 * levels, along),
    )
    incoming = lax.all_to_all(
        outgoing.reshape(owners, 1, CAP * FIELDS * lanes), ("gx", "gy"), split_axis=0, concat_axis=0, tiled=True
    ).reshape(owners * CAP * FIELDS, lanes)
    fields, inner_y, outer_y, inner_x, outer_x = deposit(
        incoming, fluid_mass.reshape(levels, along), fluid_momentum.reshape(3 * levels, along)
    )

    def swap(value, axis, outer):
        return lax.ppermute(value, ("gx", "gy"), swaps(axis, outer, sizes))

    inner_y = swap(inner_y, 1, False)
    outer_y = swap(outer_y, 1, True)
    inner_x = swap(inner_x, 0, False)
    outer_x = swap(outer_x, 0, True)
    columns = jnp.concatenate([inner_y, outer_y], axis=0)
    inner_c = swap(columns, 0, False)
    outer_c = swap(columns, 0, True)
    vmem = pl.BlockSpec(memory_space=pltpu.MemorySpace.VMEM)
    velocity, pressure = pl.pallas_call(
        functools.partial(solve_kernel, sizes),
        out_shape=(
            jax.ShapeDtypeStruct((3 * levels, along), jnp.float32),
            jax.ShapeDtypeStruct((levels, along), jnp.float32),
        ),
        in_specs=[vmem] * 7,
        out_specs=(pl.BlockSpec(memory_space=pltpu.MemorySpace.HBM), vmem),
        scratch_shapes=[pltpu.SemaphoreType.DMA],
        compiler_params=pltpu.CompilerParams(vmem_limit_bytes=8 << 20),
        name="solve",
    )(fields, inner_y, outer_y, inner_x, outer_x, inner_c, outer_c)
    return velocity.reshape(3, across, depth, along), pressure.reshape(across, depth, along)


def solution(mesh):
    return jax.shard_map(
        local,
        mesh=mesh,
        in_specs=(
            P(("gx", "gy"), None),
            P(("gx", "gy")),
            P(("gx", "gy"), None),
            P(("gx", "gy"), None),
            P(("gx", "gy"), None),
            P(("gx", "gy"), None, None),
            P(None, "gx", None, "gy"),
            P("gx", None, "gy"),
            P(None, "gx", None, "gy"),
        ),
        out_specs=(P(None, "gx", None, "gy"), P("gx", None, "gy")),
        check_vma=False,
    )
```
